512 devices in a mesh: rows: 128 (over x, z, core), rep: 4 (over y).
Axes of the slice: x: 4, y: 4, z: 16, core: 2. Of those that a mesh axis runs over, the one named last changes fastest.
Arguments:
- feats: bfloat16 [4, 32768, 512], P('rep', 'rows'), may hold values from -24 to 24
- grad_out: bfloat16 [4, 32768, 512], P('rep', 'rows'), may hold values from -6 to 6
- qkv_weight: bfloat16 [512, 1536], P('rows'), may hold values from -0.25 to 0.25
- proj_weight: bfloat16 [512, 512], P('rows'), may hold values from -0.25 to 0.25
- to_hilbert: int32 [4, 16384], P('rep', 'rows'), may hold values from 0 to 16383, as said below
- to_zorder: int32 [4, 16384], P('rep', 'rows'), may hold values from 0 to 16383, as said below
Outputs:
- grad_feats: bfloat16 [4, 32768, 512], P('rep', 'rows')
- qkv_grad: float32 [512, 1536], P('rows')
- proj_grad: float32 [512, 512], P('rows')
The draws below stay inside these ranges and needn't reach their ends.
Inputs may be any that keep to these rules, and one draw needn't show every extreme that they name: to_hilbert[s] is a permutation of the blocks of scene s and to_zorder[s] its inverse; of the 128 Z-order blocks of one device, at most 2 have Hilbert positions on any one device, and exactly 2 for some pair of devices in every scene. `to_zorder`: the inverse of to_hilbert in every scene.
All inputs are finite; a program needn't handle non-finite values.
Results may differ from the reference program's by a relative error of at most 0.015.
The reference program's roundings to bfloat16 on the way (of `qkv`, `grad_hil`, `grad_attn`, `probs_b`, `attn`, `dscore`, `grad_qkv` and `grad_hfeat`) count: a program that leaves them out, or rounds other values in their place, can miss the bound.
Values may be sent and summed in bfloat16 or wider, within the bound.
No kernel may reach another device: no remote copies, remote signals or barrier semaphores. Data moves between devices by JAX's collectives and lax.ppermute only.
A program may use at most 64 MiB of HBM per device.

```python
import jax
import jax.numpy as jnp
from jax import lax

C = 512
HEADS = 8
HD = 64
PATCH = 512
BLK = 2
POINTS = 32768
BLOCKS = 16384
SCENES = 4
N_ROWS = 128


def block_orders(key):
    peers = N_ROWS

    def one_scene(scene_key):
        key_shift, key_rot, key_slot = jax.random.split(scene_key, 3)
        chosen = jax.random.permutation(key_shift, peers)
        quarter = peers // 4
        half = peers // 2
        shifts = jnp.concatenate([chosen[:quarter], chosen[:quarter], chosen[quarter:quarter + half]])
        rotation = jax.random.randint(key_rot, (peers,), 0, peers)
        source = jnp.arange(peers, dtype=jnp.int32)[:, None]
        column = jnp.arange(peers, dtype=jnp.int32)[None, :]
        target = (source + shifts[(column + rotation[:, None]) % peers]) % peers
        flat = target.reshape(-1).astype(jnp.int32)
        order = jnp.argsort(flat, stable=True)
        position = jnp.zeros(peers * peers, jnp.int32).at[order].set(jnp.arange(peers * peers, dtype=jnp.int32))
        rank_in = position - flat * peers
        slot_keys = jax.random.split(key_slot, peers)
        shuffles = jax.vmap(lambda inner: jax.random.permutation(inner, peers))(slot_keys).astype(jnp.int32)
        forward_list = flat * peers + shuffles[flat, rank_in]
        inverse_list = jnp.zeros(peers * peers, jnp.int32).at[forward_list].set(jnp.arange(peers * peers, dtype=jnp.int32))
        return (forward_list, inverse_list)
    scene_keys = jax.random.split(key, SCENES)
    return jax.vmap(one_scene)(scene_keys)


def draw_to_hilbert(key, part):
    return block_orders(jax.random.fold_in(key, 7))[0]


def draw_to_zorder(key, part):
    return block_orders(jax.random.fold_in(key, 7))[1]


def draw_feats(key, part):
    key_main = jax.random.fold_in(key, 0)
    values = jnp.clip(jax.random.normal(key_main, (SCENES, POINTS, C), jnp.float32), -4.0, 4.0)
    return values.astype(jnp.bfloat16)


def block_scale(rng, extent, cuts, smallest, top_value):
    def one(dim, shards_of):
        steps = jax.random.uniform(jax.random.fold_in(jax.random.fold_in(rng, 6), dim), (shards_of,), jnp.float32, smallest / len(cuts), top_value / len(cuts))
        return jnp.repeat(jnp.exp(steps), extent[dim] // shards_of).reshape((-1,) + (1,) * (len(extent) - dim - 1))

    gain = one(*cuts[0])
    for cut in cuts[1:]:
        gain = gain * one(*cut)
    return gain


def noise(stream_key, dims, width, most, shards=(), kind=jnp.bfloat16):
    entries = width * jax.random.normal(stream_key, dims, jnp.float32)
    if shards:
        entries = entries * block_scale(stream_key, dims, shards, -0.22, 0.18)
    return jnp.clip(entries, -most, most).astype(kind)


def setup_inputs(seed: int = 0) -> dict:
    splits = jax.random.split(jax.random.key(seed), 7)
    feats = draw_feats(jax.random.fold_in(splits[6], 71), 0)
    grad_out = noise(splits[1], (SCENES, POINTS, C), 1.0, 6.0, ((0, 4), (1, 128)))
    qkv_weight = noise(splits[2], (C, 3 * C), C ** -0.5, 0.25, ((0, 128),))
    proj_weight = noise(splits[3], (C, C), C ** -0.5, 0.25, ((0, 128),))
    to_hilbert = draw_to_hilbert(jax.random.fold_in(splits[6], 71), 0)
    to_zorder = draw_to_zorder(jax.random.fold_in(splits[6], 71), 0)
    return {"feats": feats, "grad_out": grad_out, "qkv_weight": qkv_weight, "proj_weight": proj_weight, "to_hilbert": to_hilbert, "to_zorder": to_zorder}


def patch_backward(qkv_patch, grad_patch):
    scale = HD ** -0.5
    qf = qkv_patch[:, :C].astype(jnp.float32).reshape(PATCH, HEADS, HD)
    kf = qkv_patch[:, C:2 * C].astype(jnp.float32).reshape(PATCH, HEADS, HD)
    vf = qkv_patch[:, 2 * C:].astype(jnp.float32).reshape(PATCH, HEADS, HD)
    gf = grad_patch.astype(jnp.float32).reshape(PATCH, HEADS, HD)
    score = jnp.einsum('qhd,khd->hqk', qf, kf) * scale
    row_max = jnp.max(score, axis=-1, keepdims=True)
    raised = jnp.exp(score - row_max)
    row_sum = jnp.sum(raised, axis=-1, keepdims=True)
    probs = raised / row_sum
    probs_b = probs.astype(jnp.bfloat16).astype(jnp.float32)
    attn = jnp.einsum('hqk,khd->qhd', probs_b, vf).astype(jnp.bfloat16).reshape(PATCH, C)
    dprob = jnp.einsum('qhd,khd->hqk', gf, vf)
    delta = jnp.sum(probs * dprob, axis=-1, keepdims=True)
    dscore = (probs * (dprob - delta) * scale).astype(jnp.bfloat16).astype(jnp.float32)
    grad_q = jnp.einsum('hqk,khd->qhd', dscore, kf).reshape(PATCH, C)
    grad_k = jnp.einsum('hqk,qhd->khd', dscore, qf).reshape(PATCH, C)
    grad_v = jnp.einsum('hqk,qhd->khd', probs_b, gf).reshape(PATCH, C)
    grad_qkv = jnp.concatenate([grad_q, grad_k, grad_v], axis=1).astype(jnp.bfloat16)
    return attn, grad_qkv


def scene_backward(feat, grad_z, forward_list, inverse_list, qkv_weight, proj_weight):
    grad_hil = grad_z.reshape(BLOCKS, BLK * C)[inverse_list].reshape(POINTS, C)
    qkv = jnp.dot(feat, qkv_weight, preferred_element_type=jnp.float32).astype(jnp.bfloat16)
    grad_attn = jnp.dot(grad_hil, proj_weight.T, preferred_element_type=jnp.float32).astype(jnp.bfloat16)
    patches = POINTS // PATCH
    attn, grad_qkv = lax.map(lambda pair: patch_backward(pair[0], pair[1]),
                             (qkv.reshape(patches, PATCH, 3 * C), grad_attn.reshape(patches, PATCH, C)))
    attn = attn.reshape(POINTS, C)
    grad_qkv = grad_qkv.reshape(POINTS, 3 * C)
    grad_hfeat = jnp.dot(grad_qkv, qkv_weight.T, preferred_element_type=jnp.float32).astype(jnp.bfloat16)
    grad_feat = grad_hfeat.reshape(BLOCKS, BLK * C)[forward_list].reshape(POINTS, C)
    qkv_term = jnp.dot(feat.T, grad_qkv, preferred_element_type=jnp.float32)
    proj_term = jnp.dot(attn.T, grad_hil, preferred_element_type=jnp.float32)
    return grad_feat, qkv_term, proj_term


def reference(feats, grad_out, qkv_weight, proj_weight, to_hilbert, to_zorder):
    grads = []
    qkv_grad = jnp.zeros((C, 3 * C), jnp.float32)
    proj_grad = jnp.zeros((C, C), jnp.float32)
    for scene in range(SCENES):
        grad_feat, qkv_term, proj_term = scene_backward(feats[scene], grad_out[scene], to_hilbert[scene],
                                                        to_zorder[scene], qkv_weight, proj_weight)
        grads.append(grad_feat)
        qkv_grad = qkv_grad + qkv_term
        proj_grad = proj_grad + proj_term
    return jnp.stack(grads, axis=0), qkv_grad, proj_grad
```

```python
import jax
import jax.numpy as jnp
from jax import lax
from jax.sharding import Mesh
from jax.sharding import PartitionSpec as P

HEADS = 8
CAP = 2
BLK = 2
Z_SIZE = 16
CORES = 2
ROWS = ("x", "z", "core")
NEAR = ("x", "core", "rep")


def mm(left, right, dims, out=jnp.float32):
    res = lax.dot_general(left, right, (dims, ((), ())), preferred_element_type=jnp.float32)
    return res.astype(out)


NN = ((1,), (0,))
NT = ((1,), (1,))
TN = ((0,), (0,))


def swap(block, axis, parts):
    return lax.all_to_all(block, axis, split_axis=0, concat_axis=0, tiled=True)


def rank_within(order_keys, owners):
    same_owner = owners[None, :] == owners[:, None]
    earlier = order_keys[None, :] < order_keys[:, None]
    return jnp.sum(jnp.logical_and(same_owner, earlier).astype(jnp.int32), axis=1)


def slot_tables(owners, ranks, count):
    base = owners * (2 * CAP * BLK) + ranks * BLK
    rows = (base[:, None] + jnp.arange(BLK, dtype=jnp.int32)[None, :]).reshape(-1)
    slots = jnp.arange(count * 2 * CAP * BLK, dtype=jnp.int32)
    return [
        (slots[:, None] == (rows + half * CAP * BLK)[None, :]).astype(jnp.bfloat16)
        for half in range(2)
    ]


def per_device(feats, grad_out, qkv_weight, proj_weight, to_hilbert, to_zorder):
    bf = jnp.bfloat16
    nx, nz, nc, nr = (lax.axis_size(a) for a in ("x", "z", "core", "rep"))
    peers = nx * nz * nc
    core = lax.axis_index("core")
    rep = lax.axis_index("rep")
    feature = feats[0]
    rows_dev, channels = feature.shape
    own = channels // nc
    head_size = channels // HEADS
    heads_own = HEADS // nc
    scale = head_size ** (-0.5)
    share = qkv_weight.shape[0]
    per = share // nr
    wide = 4 * channels
    blocks_dev = to_hilbert.shape[1]

    both = jnp.concatenate([qkv_weight, proj_weight], axis=1)
    mine = lax.dynamic_slice_in_dim(both, rep * per, per, 0)
    mine = jnp.broadcast_to(mine.reshape(1, per * wide // 256, 256), (nz, per * wide // 256, 256))
    plane = swap(mine, "z", nz).reshape(nz * per, wide)
    views = []
    for c in range(nc):
        cols = [plane[:, part * channels + c * own : part * channels + (c + 1) * own] for part in range(3)]
        views.append(jnp.concatenate(cols + [plane[:, 3 * channels :]], axis=1))
    width = 3 * own + channels
    views = jnp.stack(views, axis=0)
    views = jnp.broadcast_to(views[None, :, None], (nx, nc, nr, nz * per, width))
    weights = swap(views.reshape(nx * nc * nr, nz * per, width), NEAR, None).reshape(channels, width)

    ids = jnp.arange(blocks_dev, dtype=jnp.int32)
    target = to_hilbert[0] // blocks_dev
    send = slot_tables(target, rank_within(ids, target), peers)
    source = to_zorder[0] // blocks_dev
    recv = slot_tables(source, rank_within(to_zorder[0], source), peers)
    half = channels // 2
    grad_z_in = grad_out[0]
    chunk = 2 * CAP * BLK
    outgoing = (mm(send[0], grad_z_in[:, :half], NN) + mm(send[1], grad_z_in[:, half:], NN)).astype(bf)
    arrived = swap(outgoing.reshape(peers, chunk, half), ROWS, None).reshape(peers * chunk, half)
    grad_hil = jnp.concatenate([mm(recv[h], arrived, TN, bf) for h in range(2)], axis=1)

    nat = jnp.arange(channels, dtype=jnp.int32)
    place = nat % per
    r_of = nat // per % nr
    c_of = nat // share % nc
    z_of = nat // (share * nc) % nz
    x_of = nat // (share * nc * nz)
    pos = (((x_of * nc + c_of) * nr + r_of) * nz + z_of) * per + place
    perm = (pos[:, None] == nat[None, :]).astype(bf)
    pos_own = lax.dynamic_slice_in_dim(pos, core * own, own, 0)
    perm_own = (pos_own[:, None] == nat[None, :]).astype(bf)

    pair = [(0, 1), (1, 0)]
    other_feat = lax.ppermute(feature, "core", pair)
    xf = mm(jnp.concatenate([feature, other_feat], axis=0), perm, NN, bf)
    w_qkv = weights[:, : 3 * own]
    w_proj = mm(perm_own, weights[:, 3 * own :], NN, bf)
    qkv = mm(xf, w_qkv, NN, bf)
    other_grad = lax.ppermute(grad_hil, "core", pair)
    grad_pair = jnp.concatenate([grad_hil, other_grad], axis=0)
    grad_attn = mm(grad_pair, w_proj, NT, bf)

    attn_parts, dq_parts, dk_parts, dv_parts = ([], [], [], [])
    for head_index in range(heads_own):
        lo = head_index * head_size
        q_head = qkv[:, lo : lo + head_size]
        k_head = qkv[:, own + lo : own + lo + head_size]
        v_head = qkv[:, 2 * own + lo : 2 * own + lo + head_size]
        g_head = grad_attn[:, lo : lo + head_size]
        score = mm(q_head, k_head, NT) * scale
        row_max = jnp.max(score, axis=1, keepdims=True)
        raised = jnp.exp(score - row_max)
        row_sum = jnp.sum(raised, axis=1, keepdims=True)
        probs = raised / row_sum
        probs_b = probs.astype(bf)
        attn_parts.append(mm(probs_b, v_head, NN, bf))
        dprob = mm(g_head, v_head, NT)
        delta = jnp.sum(probs * dprob, axis=1, keepdims=True)
        dscore = (probs * (dprob - delta) * scale).astype(bf)
        dq_parts.append(mm(dscore, k_head, NN, bf))
        dk_parts.append(mm(dscore, q_head, TN, bf))
        dv_parts.append(mm(probs_b, g_head, TN, bf))
    grad_qkv = jnp.concatenate(dq_parts + dk_parts + dv_parts, axis=1)
    attn = jnp.concatenate(attn_parts, axis=1)

    partial = mm(grad_qkv, w_qkv, NT)
    from_other = lax.ppermute(partial[rows_dev:].astype(bf), "core", pair)
    grad_hfeat = (partial[:rows_dev] + from_other.astype(jnp.float32)).astype(bf)
    going = (mm(recv[0], grad_hfeat[:, :half], NN) + mm(recv[1], grad_hfeat[:, half:], NN)).astype(bf)
    returned = swap(going.reshape(peers, chunk, half), ROWS, None).reshape(peers * chunk, half)
    grad_perm = jnp.concatenate([mm(send[h], returned, TN, bf) for h in range(2)], axis=1)
    grad_z = mm(grad_perm, perm, NT, bf)

    qkv_term = mm(xf, grad_qkv, TN, bf)
    attn_perm = mm(attn, perm_own, NN, bf)
    proj_term = mm(attn_perm, grad_pair, TN, bf)
    term = jnp.concatenate([qkv_term, proj_term], axis=1)
    near = swap(term.reshape(nx * nc * nr, nz * per, width), NEAR, None)
    near = near.reshape(nx, nc, nr, nz * per, width).astype(jnp.float32)
    near_qkv = jnp.sum(near[..., : 3 * own], axis=(0, 2))
    near_proj = jnp.sum(near[..., 3 * own :], axis=(0, 1, 2))
    pieces = []
    for part in range(3):
        for c in range(nc):
            pieces.append(near_qkv[c, :, part * own : (part + 1) * own])
    rows = jnp.concatenate(pieces + [near_proj], axis=1).astype(bf)
    line = per * wide // 256
    far = swap(rows.reshape(nz, line, 256), "z", nz)
    summed = jnp.sum(far.astype(jnp.float32), axis=0)
    last = swap(jnp.broadcast_to(summed[None], (nr, line, 256)), "rep", nr)
    owned = last.reshape(share, wide)
    return (grad_z[None], owned[:, : 3 * channels], owned[:, 3 * channels :])


def solution(mesh):
    rows, reps = mesh.devices.shape
    fine = Mesh(
        mesh.devices.reshape(rows // (Z_SIZE * CORES), Z_SIZE, CORES, reps),
        ("x", "z", "core", "rep"),
    )
    placed = (
        P("rep", ROWS, None),
        P("rep", ROWS, None),
        P(ROWS, None),
        P(ROWS, None),
        P("rep", ROWS),
        P("rep", ROWS),
    )
    return jax.shard_map(
        per_device,
        mesh=fine,
        in_specs=placed,
        out_specs=(P("rep", ROWS, None), P(ROWS, None), P(ROWS, None)),
        check_vma=False,
    )
```

```python
import jax
import jax.numpy as jnp
from jax import lax
from jax.experimental import pallas as pl
from jax.experimental.pallas import tpu as pltpu
from jax.sharding import Mesh
from jax.sharding import PartitionSpec as P

HEADS = 8
CAP = 2
BLK = 2
Z_HIGH = 4
Z_LOW = 4
CORES = 2
ROWS = ("x", "zh", "zl", "core")
INTERPRET = False
NN = ((1,), (0,))
NT = ((1,), (1,))
TN = ((0,), (0,))


def mm(left, right, dims, out=jnp.float32):
    res = lax.dot_general(left, right, (dims, ((), ())), preferred_element_type=jnp.float32)
    return res.astype(out)


def rank_within(order_keys, owners):
    same_owner = owners[None, :] == owners[:, None]
    earlier = order_keys[None, :] < order_keys[:, None]
    return jnp.sum(jnp.logical_and(same_owner, earlier).astype(jnp.int32), axis=1)


def slot_tables(owners, ranks, count):
    base = owners * (2 * CAP * BLK) + ranks * BLK
    rows = (base[:, None] + jnp.arange(BLK, dtype=jnp.int32)[None, :]).reshape(-1)
    slots = jnp.arange(count * 2 * CAP * BLK, dtype=jnp.int32)
    return [
        (slots[:, None] == (rows + half * CAP * BLK)[None, :]).astype(jnp.bfloat16)
        for half in range(2)
    ]


def swap(block, axis):
    return lax.all_to_all(block, axis, split_axis=0, concat_axis=0, tiled=True)


def shift(block, axis, step):
    count = lax.axis_size(axis)
    return lax.ppermute(block, axis, [(here, (here + step) % count) for here in range(count)])


def attend(qkv, grad_attn, own, head_size):
    bf = jnp.bfloat16
    rows = qkv.shape[0]
    scale = head_size ** (-0.5)
    query, key, value = qkv[:, :own], qkv[:, own : 2 * own], qkv[:, 2 * own :]
    key_t, value_t = key.T, value.T
    two = 2 * head_size
    first = lax.broadcasted_iota(jnp.int32, (rows, two), 1) < head_size
    attn_t, dq_t, dk, dv = [], [], [], []
    for pair in range(own // two):
        cols = slice(pair * two, (pair + 1) * two)
        q_pair, k_pair, v_pair, g_pair = query[:, cols], key[:, cols], value[:, cols], grad_attn[:, cols]
        zero = jnp.zeros_like(k_pair)
        dk_pair, dv_pair = [], []
        for member in range(2):
            k_head = jnp.where(first, k_pair, zero) if member == 0 else jnp.where(first, zero, k_pair)
            v_head = jnp.where(first, v_pair, zero) if member == 0 else jnp.where(first, zero, v_pair)
            score = mm(k_head, q_pair, NT)
            raised = jnp.exp((score - jnp.max(score, axis=0, keepdims=True)) * scale)
            probs = raised * (1.0 / jnp.sum(raised, axis=0, keepdims=True))
            probs_b = probs.astype(bf)
            dprob = mm(v_head, g_pair, NT)
            delta = jnp.sum(probs * dprob, axis=0, keepdims=True)
            dscore = (probs * (dprob - delta) * scale).astype(bf)
            lo = pair * two + member * head_size
            attn_t.append(mm(value_t[lo : lo + head_size], probs_b, NN, bf))
            dq_t.append(mm(key_t[lo : lo + head_size], dscore, NN, bf))
            dk_pair.append(mm(dscore, q_pair, NN))
            dv_pair.append(mm(probs_b, g_pair, NN))
        dk.append(jnp.where(first, dk_pair[0], dk_pair[1]).astype(bf))
        dv.append(jnp.where(first, dv_pair[0], dv_pair[1]).astype(bf))
    grad_q = jnp.concatenate(dq_t, axis=0).T
    return jnp.concatenate(attn_t, axis=0), jnp.concatenate([grad_q] + dk + dv, axis=1)


def patch_body(
    core_ref, x_ref, mine_ref, recv_ref, gown_ref, goth_ref, own_perm_ref,
    pown_ref, poth_ref, keep_ref, send_ref, w_ref, tq_ref, tp_ref,
):
    bf = jnp.bfloat16
    core = core_ref[0]
    channels = x_ref.shape[1]
    own = channels // CORES
    rows = gown_ref.shape[0]
    part = own // CORES
    w_ref[core] = mine_ref[...]
    w_ref[1 - core] = recv_ref[...]
    w_qkv = jnp.concatenate([w_ref[c, :, : 3 * own] for c in range(CORES)], axis=0)
    lo = pl.multiple_of(core * part, part)
    w_proj = jnp.concatenate([w_ref[c, pl.ds(lo, part), 3 * own :] for c in range(CORES)], axis=0)
    own_perm = own_perm_ref[...]
    w_proj = mm(own_perm, w_proj, NN, bf)
    x = x_ref[...]
    grad_pair = jnp.concatenate([gown_ref[...], goth_ref[...]], axis=0)
    qkv = mm(x, w_qkv, NN, bf)
    grad_attn = mm(grad_pair, w_proj, NT, bf)
    attn_t, grad_qkv = attend(qkv, grad_attn, own, channels // HEADS)
    tq_ref[...] = mm(x, grad_qkv, TN, bf).reshape(CORES, own, 3 * own)
    proj_term = mm(attn_t, grad_pair, NN, bf)
    tp_ref[...] = mm(own_perm, proj_term, TN, bf).reshape(CORES, part, channels)
    for out_ref, side in ((keep_ref, core), (send_ref, 1 - core)):
        out_ref[:, : 3 * own] = tq_ref[side]
        out_ref[:part, 3 * own :] = tp_ref[side, :, :own]
        out_ref[part:, 3 * own :] = tp_ref[side, :, own:]
    partial = mm(grad_qkv, w_qkv, NT)
    pown_ref[...] = partial[:rows]
    poth_ref[...] = partial[rows:].astype(bf)


def patch_step(core, x, mine, recv, gown, goth, own_perm):
    bf = jnp.bfloat16
    rows, channels = gown.shape
    own = channels // CORES
    vmem = pl.BlockSpec(memory_space=pltpu.VMEM)
    return pl.pallas_call(
        patch_body,
        out_shape=[
            jax.ShapeDtypeStruct((rows, channels), jnp.float32),
            jax.ShapeDtypeStruct((rows, channels), bf),
            jax.ShapeDtypeStruct((own, 4 * own), bf),
            jax.ShapeDtypeStruct((own, 4 * own), bf),
        ],
        in_specs=[pl.BlockSpec(memory_space=pltpu.SMEM)] + [vmem] * 6,
        out_specs=[vmem] * 4,
        scratch_shapes=[
            pltpu.VMEM((CORES, own, 3 * own + channels), bf),
            pltpu.VMEM((CORES, own, 3 * own), bf),
            pltpu.VMEM((CORES, own // CORES, channels), bf),
        ],
        compiler_params=pltpu.CompilerParams(vmem_limit_bytes=48 << 20),
        interpret=INTERPRET,
    )(core.reshape(1), x, mine, recv, gown, goth, own_perm)


def per_device(feats, grad_out, qkv_weight, proj_weight, to_hilbert, to_zorder):
    bf = jnp.bfloat16
    f32 = jnp.float32
    nx, zh, zl, nc, nr = (lax.axis_size(a) for a in ("x", "zh", "zl", "core", "rep"))
    nz = zh * zl
    peers = nx * nz * nc
    x_here, zh_here, zl_here, core = (lax.axis_index(a) for a in ROWS)
    feature = feats[0]
    rows_dev, channels = feature.shape
    own = channels // nc
    part = own // nc
    half = channels // 2
    share = qkv_weight.shape[0]
    blocks_dev = to_hilbert.shape[1]
    chunk = 2 * CAP * BLK
    pair = [(0, 1), (1, 0)]

    ids = jnp.arange(blocks_dev, dtype=jnp.int32)
    target = to_hilbert[0] // blocks_dev
    send = slot_tables(target, rank_within(ids, target), peers)
    source = to_zorder[0] // blocks_dev
    recv = slot_tables(source, rank_within(to_zorder[0], source), peers)
    grad_z_in = grad_out[0]
    outgoing = (mm(send[0], grad_z_in[:, :half], NN) + mm(send[1], grad_z_in[:, half:], NN)).astype(bf)

    halves = []
    for c in range(nc):
        cols = [qkv_weight[:, p * channels + c * own : p * channels + (c + 1) * own] for p in range(3)]
        halves.append(jnp.concatenate(cols + [proj_weight[:, c * own : (c + 1) * own]], axis=1))
    piece = jnp.concatenate(halves, axis=0)
    other_feat = lax.ppermute(feature, "core", pair)
    gathered = piece
    for axis in ("zh", "zl", "x"):
        gathered = jnp.concatenate([gathered] + [shift(gathered, axis, k) for k in range(1, lax.axis_size(axis))], axis=0)

    def group_index(x, z):
        low = (zl_here - z) % zl
        high = (zh_here - z // zl) % zh
        return (((x_here - x) % nx) * zl + low) * zh + high

    a = jnp.arange(own, dtype=jnp.int32)
    i_of, z_of, x_of = a % share, a // share % nz, a // (share * nz)
    slot = jnp.arange(2 * own, dtype=jnp.int32)
    picked = []
    for h in range(2):
        place = (group_index(x_of, z_of) * 2 + h) * share + i_of
        picked.append(mm((place[:, None] == slot[None, :]).astype(bf), gathered, NN, bf))
    proj_rows = [p[:, 3 * own :] for p in picked]
    qkv_mine = jnp.where(core == 0, picked[0][:, : 3 * own], picked[1][:, : 3 * own])
    qkv_theirs = jnp.where(core == 0, picked[1][:, : 3 * own], picked[0][:, : 3 * own])
    mine = jnp.concatenate([qkv_mine] + proj_rows, axis=1)
    theirs = lax.ppermute(jnp.concatenate([qkv_theirs] + proj_rows, axis=1), "core", pair)

    def order(count):
        nat = jnp.arange(count, dtype=jnp.int32)
        i, c, z, x = nat % share, nat // share % nc, nat // (share * nc) % nz, nat // (share * nc * nz)
        pos = c * (count // nc) + (x * nz + z) * share + i
        return (pos[:, None] == nat[None, :]).astype(bf)

    perm = order(channels)
    own_perm = order(own)
    x_pair = mm(jnp.concatenate([feature, other_feat], axis=0), perm, NN, bf)
    arrived = swap(outgoing.reshape(peers, chunk, half), ROWS).reshape(peers * chunk, half)
    grad_hil = jnp.concatenate([mm(recv[h], arrived, TN, bf) for h in range(2)], axis=1)
    other_grad = lax.ppermute(grad_hil, "core", pair)
    p_own, p_other, keep, away = patch_step(core, x_pair, mine, theirs, grad_hil, other_grad, own_perm)

    from_other = lax.ppermute(p_other, "core", pair)
    grad_hfeat = (p_own + from_other.astype(f32)).astype(bf)
    going = (mm(recv[0], grad_hfeat[:, :half], NN) + mm(recv[1], grad_hfeat[:, half:], NN)).astype(bf)
    returned = swap(going.reshape(peers, chunk, half), ROWS).reshape(peers * chunk, half)

    got = lax.ppermute(away, "core", pair)
    proj_all = jnp.concatenate([keep[:, 3 * own :], got[:, 3 * own :]], axis=0)
    plane = own // nx

    def toward(step):
        x_to = (x_here + step) % nx
        first = x_to * plane
        base = (x_to // (nx // nc) + core) % nc * own + x_to % (nx // nc) * plane
        pieces = [lax.dynamic_slice_in_dim(m[:, : 3 * own], first, plane, 0) for m in (keep, got)]
        pieces += [lax.dynamic_slice_in_dim(proj_all, base + k * part, plane, 0) for k in range(2)]
        return jnp.concatenate(pieces, axis=1)

    total = toward(0).astype(f32)
    arrivals = [shift(toward(step), "x", step) for step in range(1, nx)]
    total = (total + sum(t.astype(f32) for t in arrivals)).astype(bf)
    rows_left = total.shape[0] // zh

    def toward_zh(step):
        return lax.dynamic_slice_in_dim(total, (zh_here + step) % zh * rows_left, rows_left, 0)

    arrivals = [shift(toward_zh(step), "zh", step) for step in range(1, zh)]
    total = (toward_zh(0).astype(f32) + sum(t.astype(f32) for t in arrivals)).astype(bf)
    total, returned = lax.optimization_barrier((total, returned))
    wide = 4 * channels
    last = jnp.broadcast_to(total.reshape(zl, 1, share, wide), (zl, nr, share, wide))
    last = swap(last.reshape(zl * nr, share, wide), ("zl", "rep"))
    last = jnp.sum(last.astype(f32), axis=0)
    grad_perm = jnp.concatenate([mm(send[h], returned, TN, bf) for h in range(2)], axis=1)
    grad_z = mm(grad_perm, perm, NT, bf)
    lower = jnp.where(core == 0, last[:, : 3 * own], last[:, 3 * own : 6 * own])
    upper = jnp.where(core == 0, last[:, 3 * own : 6 * own], last[:, : 3 * own])
    cols = []
    for p in range(3):
        cols += [lower[:, p * own : (p + 1) * own], upper[:, p * own : (p + 1) * own]]
    return (grad_z[None], jnp.concatenate(cols, axis=1), last[:, 6 * own :])


def solution(mesh):
    rows, reps = mesh.devices.shape
    fine = Mesh(
        mesh.devices.reshape(rows // (Z_HIGH * Z_LOW * CORES), Z_HIGH, Z_LOW, CORES, reps),
        ROWS + ("rep",),
    )
    placed = (
        P("rep", ROWS, None),
        P("rep", ROWS, None),
        P(ROWS, None),
        P(ROWS, None),
        P("rep", ROWS),
        P("rep", ROWS),
    )
    return jax.shard_map(
        per_device,
        mesh=fine,
        in_specs=placed,
        out_specs=(P("rep", ROWS, None), P(ROWS, None), P(ROWS, None)),
        check_vma=False,
    )
```

```python
import jax
import jax.numpy as jnp
from jax import lax
from jax.experimental import pallas as pl
from jax.experimental.pallas import tpu as pltpu
from jax.sharding import Mesh
from jax.sharding import PartitionSpec as P

HEADS = 8
CAP = 2
BLK = 2
Z_HIGH = 4
Z_LOW = 4
CORES = 2
ROWS = ("x", "zh", "zl", "core")
INTERPRET = False
NN = ((1,), (0,))
NT = ((1,), (1,))
TN = ((0,), (0,))


def mm(left, right, dims, out=jnp.float32):
    res = lax.dot_general(left, right, (dims, ((), ())), preferred_element_type=jnp.float32)
    return res.astype(out)


def rank_within(order_keys, owners):
    same_owner = owners[None, :] == owners[:, None]
    earlier = order_keys[None, :] < order_keys[:, None]
    return jnp.sum(jnp.logical_and(same_owner, earlier).astype(jnp.int32), axis=1)


def slot_tables(owners, ranks, count):
    base = owners * (2 * CAP * BLK) + ranks * BLK
    rows = (base[:, None] + jnp.arange(BLK, dtype=jnp.int32)[None, :]).reshape(-1)
    slots = jnp.arange(count * 2 * CAP * BLK, dtype=jnp.int32)
    return [
        (slots[:, None] == (rows + half * CAP * BLK)[None, :]).astype(jnp.bfloat16)
        for half in range(2)
    ]


def swap(block, axis):
    return lax.all_to_all(block, axis, split_axis=0, concat_axis=0, tiled=True)


def across_x(block):
    count = lax.axis_size("x")
    return lax.ppermute(block, "x", [(here, (here + count // 2) % count) for here in range(count)])


def attend(qkv, grad_attn, own, head_size):
    bf = jnp.bfloat16
    rows = qkv.shape[0]
    scale = head_size ** (-0.5)
    query, key, value = qkv[:, :own], qkv[:, own : 2 * own], qkv[:, 2 * own :]
    key_t, value_t = key.T, value.T
    two = 2 * head_size
    first = lax.broadcasted_iota(jnp.int32, (rows, two), 1) < head_size
    attn_t, dq_t, dk, dv = [], [], [], []
    for pair in range(own // two):
        cols = slice(pair * two, (pair + 1) * two)
        q_pair, k_pair, v_pair, g_pair = query[:, cols], key[:, cols], value[:, cols], grad_attn[:, cols]
        zero = jnp.zeros_like(k_pair)
        dk_pair, dv_pair = [], []
        for member in range(2):
            k_head = jnp.where(first, k_pair, zero) if member == 0 else jnp.where(first, zero, k_pair)
            v_head = jnp.where(first, v_pair, zero) if member == 0 else jnp.where(first, zero, v_pair)
            score = mm(k_head, q_pair, NT)
            raised = jnp.exp((score - jnp.max(score, axis=0, keepdims=True)) * scale)
            probs = raised * (1.0 / jnp.sum(raised, axis=0, keepdims=True))
            probs_b = probs.astype(bf)
            dprob = mm(v_head, g_pair, NT)
            delta = jnp.sum(probs * dprob, axis=0, keepdims=True)
            dscore = (probs * (dprob - delta) * scale).astype(bf)
            lo = pair * two + member * head_size
            attn_t.append(mm(value_t[lo : lo + head_size], probs_b, NN, bf))
            dq_t.append(mm(key_t[lo : lo + head_size], dscore, NN, bf))
            dk_pair.append(mm(dscore, q_pair, NN))
            dv_pair.append(mm(probs_b, g_pair, NN))
        dk.append(jnp.where(first, dk_pair[0], dk_pair[1]).astype(bf))
        dv.append(jnp.where(first, dv_pair[0], dv_pair[1]).astype(bf))
    grad_q = jnp.concatenate(dq_t, axis=0).T
    return jnp.concatenate(attn_t, axis=0), jnp.concatenate([grad_q] + dk + dv, axis=1)


def patch_body(
    core_ref, xown_ref, xoth_ref, w_ref, gown_ref, goth_ref, pown_ref, poth_ref, term_ref
):
    bf = jnp.bfloat16
    core = core_ref[0]
    rows, channels = gown_ref.shape
    own = channels // CORES
    first = pl.multiple_of(core * own, own)
    second = pl.multiple_of((1 - core) * own, own)
    w_qkv = jnp.concatenate([w_ref[p] for p in range(3)], axis=1)
    w_proj = jnp.concatenate([w_ref[3, pl.ds(first, own), :], w_ref[3, pl.ds(second, own), :]], axis=1)
    x = jnp.concatenate([xown_ref[...], xoth_ref[...]], axis=0)
    grad_pair = jnp.concatenate([gown_ref[...], goth_ref[...]], axis=0)
    qkv = mm(x, w_qkv, NN, bf)
    grad_attn = mm(grad_pair, w_proj, NT, bf)
    attn_t, grad_qkv = attend(qkv, grad_attn, own, channels // HEADS)
    qkv_term = mm(x, grad_qkv, TN, bf)
    for p in range(3):
        term_ref[p] = qkv_term[:, p * own : (p + 1) * own]
    proj_term = mm(attn_t, grad_pair, NN, bf)
    term_ref[3, pl.ds(first, own), :] = proj_term[:, :own]
    term_ref[3, pl.ds(second, own), :] = proj_term[:, own:]
    partial = mm(grad_qkv, w_qkv, NT)
    pown_ref[...] = partial[:rows]
    poth_ref[...] = partial[rows:].astype(bf)


def patch_step(core, xown, xoth, weights, gown, goth):
    bf = jnp.bfloat16
    rows, channels = gown.shape
    vmem = pl.BlockSpec(memory_space=pltpu.VMEM)
    return pl.pallas_call(
        patch_body,
        out_shape=[
            jax.ShapeDtypeStruct((rows, channels), jnp.float32),
            jax.ShapeDtypeStruct((rows, channels), bf),
            jax.ShapeDtypeStruct(weights.shape, bf),
        ],
        in_specs=[pl.BlockSpec(memory_space=pltpu.SMEM)] + [vmem] * 5,
        out_specs=[vmem] * 3,
        compiler_params=pltpu.CompilerParams(vmem_limit_bytes=48 << 20),
        interpret=INTERPRET,
    )(core.reshape(1), xown, xoth, weights, gown, goth)


def per_device(feats, grad_out, qkv_weight, proj_weight, to_hilbert, to_zorder):
    bf = jnp.bfloat16
    f32 = jnp.float32
    nx, zh, zl, nc, nr = (lax.axis_size(a) for a in ROWS + ("rep",))
    peers = nx * zh * zl * nc
    x_here, core, rep = (lax.axis_index(a) for a in ("x", "core", "rep"))
    feature = feats[0]
    rows_dev, channels = feature.shape
    own = channels // nc
    half = channels // 2
    lanes = own // 2
    share = qkv_weight.shape[0]
    blocks_dev = to_hilbert.shape[1]
    chunk = 2 * CAP * BLK
    pair = [(0, 1), (1, 0)]
    side = x_here // (nx // nc)

    partner_proj = across_x(proj_weight[:, own:])
    other_feat = lax.ppermute(feature, "core", pair)

    ids = jnp.arange(blocks_dev, dtype=jnp.int32)
    target = to_hilbert[0] // blocks_dev
    send = slot_tables(target, rank_within(ids, target), peers)
    source = to_zorder[0] // blocks_dev
    recv = slot_tables(source, rank_within(to_zorder[0], source), peers)
    grad_z_in = grad_out[0]
    outgoing = (mm(send[0], grad_z_in[:, :half], NN) + mm(send[1], grad_z_in[:, half:], NN)).astype(bf)

    parts = lax.dynamic_slice_in_dim(jnp.concatenate([qkv_weight, proj_weight], axis=1), rep * channels, channels, 1)
    riding = []
    for c in range(nc):
        piece = parts[:, c * own : (c + 1) * own]
        proj = jnp.where(side == c, proj_weight[:, :own], partner_proj)
        piece = jnp.where(rep == nr - 1, proj, piece)
        riding.append(jnp.concatenate([piece[:, :lanes], piece[:, lanes:]], axis=0))
    riding = jnp.broadcast_to(jnp.stack(riding)[None], (peers // nc, nc, 2 * share, lanes))
    both = jnp.concatenate([outgoing.reshape(peers, chunk, half), riding.reshape(peers, 2 * share, lanes)], axis=2)
    both = swap(both, ROWS)
    arrived = both[:, :, :half].reshape(peers * chunk, half)
    rode = both[:, :, half:].reshape(2 * channels, lanes)

    nat = jnp.arange(channels, dtype=jnp.int32)
    wide = jnp.arange(2 * channels, dtype=jnp.int32)
    pick = [
        ((nat // share * (2 * share) + h * share + nat % share)[:, None] == wide[None, :]).astype(bf)
        for h in range(2)
    ]
    part = jnp.concatenate([mm(pick[h], rode, NN, bf) for h in range(2)], axis=1)
    weights = swap(jnp.broadcast_to(part[None], (nr, channels, own)), "rep")

    grad_hil = jnp.concatenate([mm(recv[h], arrived, TN, bf) for h in range(2)], axis=1)
    other_grad = lax.ppermute(grad_hil, "core", pair)
    p_own, p_other, term = patch_step(core, feature, other_feat, weights, grad_hil, other_grad)

    near = jnp.sum(swap(term, "rep").astype(f32), axis=0).astype(bf)
    riding = (mm(pick[0], near[:, :lanes], TN) + mm(pick[1], near[:, lanes:], TN)).astype(bf)

    from_other = lax.ppermute(p_other, "core", pair)
    grad_hfeat = (p_own + from_other.astype(f32)).astype(bf)
    going = (mm(recv[0], grad_hfeat[:, :half], NN) + mm(recv[1], grad_hfeat[:, half:], NN)).astype(bf)
    both = jnp.concatenate([going.reshape(peers, chunk, half), riding.reshape(peers, 2 * share, lanes)], axis=2)
    both = swap(both, ROWS)
    returned = both[:, :, :half].reshape(peers * chunk, half)
    rode = both[:, :, half:].reshape(peers // nc, nc, 2 * share, lanes)
    summed = jnp.sum(rode.astype(f32), axis=0)
    last = swap(jnp.broadcast_to(summed[None], (nx * nr, nc, 2 * share, lanes)), ("x", "rep"))
    last = last.reshape(nx, nr, nc, 2, share, lanes)
    mine = lax.dynamic_index_in_dim(last, x_here, 0, keepdims=False)
    partner = lax.dynamic_index_in_dim(last, (x_here + nx // 2) % nx, 0, keepdims=False)
    cols = [mine[p, c, h] for p in range(3) for c in range(nc) for h in range(2)]
    proj = [lax.dynamic_index_in_dim(m[3], side, 0, keepdims=False) for m in (mine, partner)]
    proj_cols = [m[h] for m in proj for h in range(2)]

    grad_z = jnp.concatenate([mm(send[h], returned, TN, bf) for h in range(2)], axis=1)
    return (grad_z[None], jnp.concatenate(cols, axis=1), jnp.concatenate(proj_cols, axis=1))


def solution(mesh):
    rows, reps = mesh.devices.shape
    fine = Mesh(
        mesh.devices.reshape(rows // (Z_HIGH * Z_LOW * CORES), Z_HIGH, Z_LOW, CORES, reps),
        ROWS + ("rep",),
    )
    placed = (
        P("rep", ROWS, None),
        P("rep", ROWS, None),
        P(ROWS, None),
        P(ROWS, None),
        P("rep", ROWS),
        P("rep", ROWS),
    )
    return jax.shard_map(
        per_device,
        mesh=fine,
        in_specs=placed,
        out_specs=(P("rep", ROWS, None), P(ROWS, None), P(ROWS, None)),
        check_vma=False,
    )
```

```python
import jax
import jax.numpy as jnp
from jax import lax
from jax.experimental import pallas as pl
from jax.experimental.pallas import tpu as pltpu
from jax.sharding import Mesh
from jax.sharding import PartitionSpec as P

HEADS = 8
CAP = 2
BLK = 2
Z_HIGH = 4
Z_LOW = 4
CORES = 2
ROWS = ("x", "zh", "zl", "core")
INTERPRET = False
NN = ((1,), (0,))
NT = ((1,), (1,))
TN = ((0,), (0,))


def mm(left, right, dims, out=jnp.float32):
    res = lax.dot_general(left, right, (dims, ((), ())), preferred_element_type=jnp.float32)
    return res.astype(out)


def rank_within(order_keys, owners):
    same_owner = owners[None, :] == owners[:, None]
    earlier = order_keys[None, :] < order_keys[:, None]
    return jnp.sum(jnp.logical_and(same_owner, earlier).astype(jnp.int32), axis=1)


def slot_tables(owners, ranks, count):
    base = owners * (2 * CAP * BLK) + ranks * BLK
    rows = (base[:, None] + jnp.arange(BLK, dtype=jnp.int32)[None, :]).reshape(-1)
    slots = jnp.arange(count * 2 * CAP * BLK, dtype=jnp.int32)
    return [
        (slots[:, None] == (rows + half * CAP * BLK)[None, :]).astype(jnp.bfloat16)
        for half in range(2)
    ]


def swap(block, axis):
    return lax.all_to_all(block, axis, split_axis=0, concat_axis=0, tiled=True)


def shift(block, axis, step):
    count = lax.axis_size(axis)
    return lax.ppermute(block, axis, [(here, (here + step) % count) for here in range(count)])


def flip(block, axis, bit):
    count = lax.axis_size(axis)
    return lax.ppermute(block, axis, [(here, here ^ bit) for here in range(count)])


def attend(qkv, grad_attn, own, head_size):
    bf = jnp.bfloat16
    rows = qkv.shape[0]
    scale = head_size ** (-0.5)
    query, key, value = qkv[:, :own], qkv[:, own : 2 * own], qkv[:, 2 * own :]
    key_t, value_t = key.T, value.T
    two = 2 * head_size
    first = lax.broadcasted_iota(jnp.int32, (rows, two), 1) < head_size
    attn_t, dq_t, dk, dv = [], [], [], []
    for pair in range(own // two):
        cols = slice(pair * two, (pair + 1) * two)
        q_pair, k_pair, v_pair, g_pair = query[:, cols], key[:, cols], value[:, cols], grad_attn[:, cols]
        zero = jnp.zeros_like(k_pair)
        dk_pair, dv_pair = [], []
        for member in range(2):
            k_head = jnp.where(first, k_pair, zero) if member == 0 else jnp.where(first, zero, k_pair)
            v_head = jnp.where(first, v_pair, zero) if member == 0 else jnp.where(first, zero, v_pair)
            score = mm(k_head, q_pair, NT)
            raised = jnp.exp((score - jnp.max(score, axis=0, keepdims=True)) * scale)
            probs = raised * (1.0 / jnp.sum(raised, axis=0, keepdims=True))
            probs_b = probs.astype(bf)
            dprob = mm(v_head, g_pair, NT)
            delta = jnp.sum(probs * dprob, axis=0, keepdims=True)
            dscore = (probs * (dprob - delta) * scale).astype(bf)
            lo = pair * two + member * head_size
            attn_t.append(mm(value_t[lo : lo + head_size], probs_b, NN, bf))
            dq_t.append(mm(key_t[lo : lo + head_size], dscore, NN, bf))
            dk_pair.append(mm(dscore, q_pair, NN))
            dv_pair.append(mm(probs_b, g_pair, NN))
        dk.append(jnp.where(first, dk_pair[0], dk_pair[1]).astype(bf))
        dv.append(jnp.where(first, dv_pair[0], dv_pair[1]).astype(bf))
    grad_q = jnp.concatenate(dq_t, axis=0).T
    return jnp.concatenate(attn_t, axis=0), jnp.concatenate([grad_q] + dk + dv, axis=1)


def patch_body(
    place_ref, x_ref, w0_ref, w1_ref, w2_ref, w3_ref, gown_ref, goth_ref, own_perm_ref,
    pown_ref, poth_ref, keep_ref, send_ref, w_ref, tq_ref, tp_ref,
):
    bf = jnp.bfloat16
    core, rep = place_ref[0], place_ref[1]
    channels = x_ref.shape[1]
    own = channels // CORES
    rows = gown_ref.shape[0]
    part = own // CORES
    for k, ref in enumerate((w0_ref, w1_ref, w2_ref, w3_ref)):
        slot = lax.rem(rep + 4 - k, 4)
        w_ref[slot, core] = ref[:own]
        w_ref[slot, 1 - core] = ref[own:]
    w_qkv = jnp.concatenate([w_ref[p].reshape(channels, own) for p in range(3)], axis=1)
    cols = [
        jnp.concatenate([w_ref[3, c, h * part : (h + 1) * part] for c in range(CORES)], axis=0) for h in range(2)
    ]
    own_perm = own_perm_ref[...]
    w_proj = mm(own_perm, jnp.concatenate(cols, axis=1), NN, bf)
    x = x_ref[...]
    grad_pair = jnp.concatenate([gown_ref[...], goth_ref[...]], axis=0)
    qkv = mm(x, w_qkv, NN, bf)
    grad_attn = mm(grad_pair, w_proj, NT, bf)
    attn_t, grad_qkv = attend(qkv, grad_attn, own, channels // HEADS)
    tq_ref[...] = mm(x, grad_qkv, TN, bf).reshape(CORES, own, 3 * own)
    proj_term = mm(attn_t, grad_pair, NN, bf)
    tp_ref[...] = mm(own_perm, proj_term, TN, bf).reshape(CORES, part, channels)
    for out_ref, side in ((keep_ref, core), (send_ref, 1 - core)):
        out_ref[:, : 3 * own] = tq_ref[side]
        out_ref[:part, 3 * own :] = tp_ref[side, :, :own]
        out_ref[part:, 3 * own :] = tp_ref[side, :, own:]
    partial = mm(grad_qkv, w_qkv, NT)
    pown_ref[...] = partial[:rows]
    poth_ref[...] = partial[rows:].astype(bf)


def patch_step(place, x, weights, gown, goth, own_perm):
    bf = jnp.bfloat16
    rows, channels = gown.shape
    own = channels // CORES
    vmem = pl.BlockSpec(memory_space=pltpu.VMEM)
    return pl.pallas_call(
        patch_body,
        out_shape=[
            jax.ShapeDtypeStruct((rows, channels), jnp.float32),
            jax.ShapeDtypeStruct((rows, channels), bf),
            jax.ShapeDtypeStruct((own, 4 * own), bf),
            jax.ShapeDtypeStruct((own, 4 * own), bf),
        ],
        in_specs=[pl.BlockSpec(memory_space=pltpu.SMEM)] + [vmem] * 8,
        out_specs=[vmem] * 4,
        scratch_shapes=[
            pltpu.VMEM((4, CORES, own, own), bf),
            pltpu.VMEM((CORES, own, 3 * own), bf),
            pltpu.VMEM((CORES, own // CORES, channels), bf),
        ],
        compiler_params=pltpu.CompilerParams(vmem_limit_bytes=48 << 20),
        interpret=INTERPRET,
    )(place, x, *weights, gown, goth, own_perm)


def per_device(feats, grad_out, qkv_weight, proj_weight, to_hilbert, to_zorder):
    bf = jnp.bfloat16
    f32 = jnp.float32
    nx, zh, zl, nc, nr = (lax.axis_size(a) for a in ROWS + ("rep",))
    nz = zh * zl
    peers = nx * nz * nc
    x_here, core, rep = (lax.axis_index(a) for a in ("x", "core", "rep"))
    feature = feats[0]
    rows_dev, channels = feature.shape
    own = channels // nc
    part = own // nc
    half = channels // 2
    share = qkv_weight.shape[0]
    blocks_dev = to_hilbert.shape[1]
    chunk = 2 * CAP * BLK
    pair = [(0, 1), (1, 0)]
    bits = [1 << b for b in range(nx.bit_length() - 1)]

    mine = lax.dynamic_slice_in_dim(jnp.concatenate([qkv_weight, proj_weight], axis=1), rep * channels, channels, 1)
    mine = jnp.concatenate([mine[:, :own], mine[:, own:]], axis=0)
    plane = swap(jnp.broadcast_to(mine[None], (nz, 2 * share, own)), ("zh", "zl")).reshape(nz * 2 * share, own)

    ids = jnp.arange(blocks_dev, dtype=jnp.int32)
    target = to_hilbert[0] // blocks_dev
    send = slot_tables(target, rank_within(ids, target), peers)
    source = to_zorder[0] // blocks_dev
    recv = slot_tables(source, rank_within(to_zorder[0], source), peers)
    grad_z_in = grad_out[0]
    outgoing = (mm(send[0], grad_z_in[:, :half], NN) + mm(send[1], grad_z_in[:, half:], NN)).astype(bf)
    outgoing, plane = lax.optimization_barrier((outgoing, plane))
    arrived = swap(outgoing.reshape(peers, chunk, half), ROWS).reshape(peers * chunk, half)

    gathered = plane
    for bit in bits[::-1]:
        gathered = jnp.concatenate([gathered, flip(gathered, "x", bit)], axis=0)

    def x_index(x):
        apart = x ^ x_here
        index = jnp.zeros_like(apart)
        for bit in bits:
            index = index * 2 + (apart // bit) % 2
        return index

    a = jnp.arange(own, dtype=jnp.int32)
    i_of, z_of, top = a % share, a // share % nz, a // (share * nz)
    slot = jnp.arange(2 * own, dtype=jnp.int32)
    picked = []
    for c in range(nc):
        side = nx // nc
        for_qkv = (x_index(top) * nz + z_of) * 2 + c
        for_proj = (x_index(c * side + top % side) * nz + z_of) * 2 + top // side
        place = jnp.where(rep == 3, for_proj, for_qkv) * share + i_of
        picked.append(mm((place[:, None] == slot[None, :]).astype(bf), gathered, NN, bf))
    kept = jnp.where(core == 0, picked[0], picked[1])
    theirs = lax.ppermute(jnp.where(core == 0, picked[1], picked[0]), "core", pair)
    parts = jnp.concatenate([kept, theirs], axis=0)
    weights = [parts] + [shift(parts, "rep", k) for k in range(1, nr)]

    def order(count):
        nat = jnp.arange(count, dtype=jnp.int32)
        i, c, z, x = nat % share, nat // share % nc, nat // (share * nc) % nz, nat // (share * nc * nz)
        pos = c * (count // nc) + (x * nz + z) * share + i
        return (pos[:, None] == nat[None, :]).astype(bf)

    perm = order(channels)
    own_perm = order(own)
    other_feat = lax.ppermute(feature, "core", pair)
    x_pair = mm(jnp.concatenate([feature, other_feat], axis=0), perm, NN, bf)
    grad_hil = jnp.concatenate([mm(recv[h], arrived, TN, bf) for h in range(2)], axis=1)
    other_grad = lax.ppermute(grad_hil, "core", pair)
    place = jnp.stack([core, rep])
    p_own, p_other, keep, away = patch_step(place, x_pair, weights, grad_hil, other_grad, own_perm)

    from_other = lax.ppermute(p_other, "core", pair)
    grad_hfeat = (p_own + from_other.astype(f32)).astype(bf)
    going = (mm(recv[0], grad_hfeat[:, :half], NN) + mm(recv[1], grad_hfeat[:, half:], NN)).astype(bf)
    returned = swap(going.reshape(peers, chunk, half), ROWS).reshape(peers * chunk, half)

    got = lax.ppermute(away, "core", pair)
    proj = [jnp.concatenate([m[:part, 3 * own :], m[part:, 3 * own :]], axis=1) for m in (keep, got)]
    proj = jnp.concatenate([jnp.where(core == 0, proj[0], proj[1]), jnp.where(core == 0, proj[1], proj[0])], axis=0)
    total = jnp.concatenate([keep[:, : 3 * own], got[:, : 3 * own], proj], axis=1)

    def halve(value, axis, here, bit, first, second):
        mine_set = here // bit % 2 == 1
        stay = jnp.where(mine_set, second, first)
        come = flip(jnp.where(mine_set, first, second), axis, bit)
        return (stay.astype(f32) + come.astype(f32)).astype(bf)

    for bit in bits:
        count = nx // bit
        blocks = total.reshape(count // 2, 2, nz * share, total.shape[1])
        flat = (count // 2 * nz * share, total.shape[1])
        total = halve(total, "x", x_here, bit, blocks[:, 0].reshape(flat), blocks[:, 1].reshape(flat))
    for bit in (1, 2):
        wide = total.shape[1] // 2
        total = halve(total, "rep", rep, bit, total[:, :wide], total[:, wide:])
    total, returned = lax.optimization_barrier((total, returned))
    wide = total.shape[1]
    far = swap(total.reshape(nz, share, wide), ("zh", "zl"))
    summed = jnp.sum(far.astype(f32), axis=0)
    last = swap(jnp.broadcast_to(summed[None], (nr, share, wide)), "rep")
    last = jnp.concatenate([last[r] for r in (0, 2, 1, 3)], axis=1)
    grad_perm = jnp.concatenate([mm(send[h], returned, TN, bf) for h in range(2)], axis=1)
    grad_z = mm(grad_perm, perm, NT, bf)
    lower = jnp.where(core == 0, last[:, : 3 * own], last[:, 3 * own : 6 * own])
    upper = jnp.where(core == 0, last[:, 3 * own : 6 * own], last[:, : 3 * own])
    cols = []
    for p in range(3):
        cols += [lower[:, p * own : (p + 1) * own], upper[:, p * own : (p + 1) * own]]
    return (grad_z[None], jnp.concatenate(cols, axis=1), last[:, 6 * own :])


def solution(mesh):
    rows, reps = mesh.devices.shape
    fine = Mesh(
        mesh.devices.reshape(rows // (Z_HIGH * Z_LOW * CORES), Z_HIGH, Z_LOW, CORES, reps),
        ROWS + ("rep",),
    )
    placed = (
        P("rep", ROWS, None),
        P("rep", ROWS, None),
        P(ROWS, None),
        P(ROWS, None),
        P("rep", ROWS),
        P("rep", ROWS),
    )
    return jax.shard_map(
        per_device,
        mesh=fine,
        in_specs=placed,
        out_specs=(P("rep", ROWS, None), P(ROWS, None), P(ROWS, None)),
        check_vma=False,
    )
```

```python
import jax
import jax.numpy as jnp
from jax import lax
from jax.experimental import pallas as pl
from jax.experimental.pallas import tpu as pltpu
from jax.sharding import Mesh
from jax.sharding import PartitionSpec as P

HEADS = 8
CAP = 2
BLK = 2
Z_HIGH = 4
Z_LOW = 4
CORES = 2
ROWS = ("x", "zh", "zl", "core")
INTERPRET = False
NN = ((1,), (0,))
NT = ((1,), (1,))
TN = ((0,), (0,))


def mm(left, right, dims, out=jnp.float32):
    res = lax.dot_general(left, right, (dims, ((), ())), preferred_element_type=jnp.float32)
    return res.astype(out)


def rank_within(order_keys, owners):
    same_owner = owners[None, :] == owners[:, None]
    earlier = order_keys[None, :] < order_keys[:, None]
    return jnp.sum(jnp.logical_and(same_owner, earlier).astype(jnp.int32), axis=1)


def slot_tables(owners, ranks, count):
    base = owners * (2 * CAP * BLK) + ranks * BLK
    rows = (base[:, None] + jnp.arange(BLK, dtype=jnp.int32)[None, :]).reshape(-1)
    slots = jnp.arange(count * 2 * CAP * BLK, dtype=jnp.int32)
    return [
        (slots[:, None] == (rows + half * CAP * BLK)[None, :]).astype(jnp.bfloat16)
        for half in range(2)
    ]


def swap(block, axis):
    return lax.all_to_all(block, axis, split_axis=0, concat_axis=0, tiled=True)


def shift(block, axis, step):
    count = lax.axis_size(axis)
    return lax.ppermute(block, axis, [(here, (here + step) % count) for here in range(count)])


def flip(block, axis, bit):
    count = lax.axis_size(axis)
    return lax.ppermute(block, axis, [(here, here ^ bit) for here in range(count)])


def attend(qkv, grad_attn, own, head_size):
    bf = jnp.bfloat16
    rows = qkv.shape[0]
    scale = head_size ** (-0.5)
    query, key, value = qkv[:, :own], qkv[:, own : 2 * own], qkv[:, 2 * own :]
    key_t, value_t = key.T, value.T
    two = 2 * head_size
    first = lax.broadcasted_iota(jnp.int32, (rows, two), 1) < head_size
    attn_t, dq_t, dk, dv = [], [], [], []
    for pair in range(own // two):
        cols = slice(pair * two, (pair + 1) * two)
        q_pair, k_pair, v_pair, g_pair = query[:, cols], key[:, cols], value[:, cols], grad_attn[:, cols]
        zero = jnp.zeros_like(k_pair)
        dk_pair, dv_pair = [], []
        for member in range(2):
            k_head = jnp.where(first, k_pair, zero) if member == 0 else jnp.where(first, zero, k_pair)
            v_head = jnp.where(first, v_pair, zero) if member == 0 else jnp.where(first, zero, v_pair)
            score = mm(k_head, q_pair, NT)
            raised = jnp.exp((score - jnp.max(score, axis=0, keepdims=True)) * scale)
            probs = raised * (1.0 / jnp.sum(raised, axis=0, keepdims=True))
            probs_b = probs.astype(bf)
            dprob = mm(v_head, g_pair, NT)
            delta = jnp.sum(probs * dprob, axis=0, keepdims=True)
            dscore = (probs * (dprob - delta) * scale).astype(bf)
            lo = pair * two + member * head_size
            attn_t.append(mm(value_t[lo : lo + head_size], probs_b, NN, bf))
            dq_t.append(mm(key_t[lo : lo + head_size], dscore, NN, bf))
            dk_pair.append(mm(dscore, q_pair, NN))
            dv_pair.append(mm(probs_b, g_pair, NN))
        dk.append(jnp.where(first, dk_pair[0], dk_pair[1]).astype(bf))
        dv.append(jnp.where(first, dv_pair[0], dv_pair[1]).astype(bf))
    grad_q = jnp.concatenate(dq_t, axis=0).T
    return jnp.concatenate(attn_t, axis=0), jnp.concatenate([grad_q] + dk + dv, axis=1)


def patch_body(
    place_ref, x_ref, w0_ref, w1_ref, w2_ref, w3_ref, gown_ref, goth_ref, own_perm_ref,
    pown_ref, poth_ref, term_ref, w_ref,
):
    bf = jnp.bfloat16
    core, rep = place_ref[0], place_ref[1]
    channels = x_ref.shape[1]
    own = channels // CORES
    rows = gown_ref.shape[0]
    part = own // CORES
    for k, ref in enumerate((w0_ref, w1_ref, w2_ref, w3_ref)):
        slot = lax.rem(rep + 4 - k, 4)
        w_ref[slot, core] = ref[:own]
        w_ref[slot, 1 - core] = ref[own:]
    w_qkv = jnp.concatenate([w_ref[p].reshape(channels, own) for p in range(3)], axis=1)
    cols = [
        jnp.concatenate([w_ref[3, c, h * part : (h + 1) * part] for c in range(CORES)], axis=0) for h in range(2)
    ]
    own_perm = own_perm_ref[...]
    w_proj = mm(own_perm, jnp.concatenate(cols, axis=1), NN, bf)
    x = x_ref[...]
    grad_pair = jnp.concatenate([gown_ref[...], goth_ref[...]], axis=0)
    qkv = mm(x, w_qkv, NN, bf)
    grad_attn = mm(grad_pair, w_proj, NT, bf)
    attn_t, grad_qkv = attend(qkv, grad_attn, own, channels // HEADS)
    qkv_term = mm(x, grad_qkv, TN, bf)
    proj_term = mm(own_perm, mm(attn_t, grad_pair, NN, bf), TN, bf)
    nx = term_ref.shape[0]
    tall = own // nx
    for c in range(CORES):
        for there in range(nx):
            lo = c * own + there * tall
            for p in range(3):
                term_ref[there, c, p] = qkv_term[lo : lo + tall, p * own : (p + 1) * own]
            lo = c * part + there % (nx // CORES) * tall
            block = proj_term[lo : lo + tall]
            term_ref[there, c, 3] = jnp.where(core == there // (nx // CORES), block[:, :own], block[:, own:])
    partial = mm(grad_qkv, w_qkv, NT)
    pown_ref[...] = partial[:rows]
    poth_ref[...] = partial[rows:].astype(bf)


def patch_step(place, x, weights, gown, goth, own_perm, nx):
    bf = jnp.bfloat16
    rows, channels = gown.shape
    own = channels // CORES
    vmem = pl.BlockSpec(memory_space=pltpu.VMEM)
    return pl.pallas_call(
        patch_body,
        out_shape=[
            jax.ShapeDtypeStruct((rows, channels), jnp.float32),
            jax.ShapeDtypeStruct((rows, channels), bf),
            jax.ShapeDtypeStruct((nx, CORES, 4, own // nx, own), bf),
        ],
        in_specs=[pl.BlockSpec(memory_space=pltpu.SMEM)] + [vmem] * 8,
        out_specs=[vmem] * 3,
        scratch_shapes=[
            pltpu.VMEM((4, CORES, own, own), bf),
        ],
        compiler_params=pltpu.CompilerParams(vmem_limit_bytes=48 << 20),
        interpret=INTERPRET,
    )(place, x, *weights, gown, goth, own_perm)


def per_device(feats, grad_out, qkv_weight, proj_weight, to_hilbert, to_zorder):
    bf = jnp.bfloat16
    f32 = jnp.float32
    nx, zh, zl, nc, nr = (lax.axis_size(a) for a in ROWS + ("rep",))
    nz = zh * zl
    peers = nx * nz * nc
    x_here, core, rep = (lax.axis_index(a) for a in ("x", "core", "rep"))
    feature = feats[0]
    rows_dev, channels = feature.shape
    own = channels // nc
    part = own // nc
    half = channels // 2
    share = qkv_weight.shape[0]
    blocks_dev = to_hilbert.shape[1]
    chunk = 2 * CAP * BLK
    pair = [(0, 1), (1, 0)]
    bits = [1 << b for b in range(nx.bit_length() - 1)]

    mine = lax.dynamic_slice_in_dim(jnp.concatenate([qkv_weight, proj_weight], axis=1), rep * channels, channels, 1)
    mine = jnp.concatenate([mine[:, :own], mine[:, own:]], axis=0)
    plane = swap(jnp.broadcast_to(mine[None], (nz, 2 * share, own)), ("zh", "zl")).reshape(nz * 2 * share, own)

    ids = jnp.arange(blocks_dev, dtype=jnp.int32)
    target = to_hilbert[0] // blocks_dev
    send = slot_tables(target, rank_within(ids, target), peers)
    source = to_zorder[0] // blocks_dev
    recv = slot_tables(source, rank_within(to_zorder[0], source), peers)
    grad_z_in = grad_out[0]
    outgoing = (mm(send[0], grad_z_in[:, :half], NN) + mm(send[1], grad_z_in[:, half:], NN)).astype(bf)
    outgoing, plane = lax.optimization_barrier((outgoing, plane))
    arrived = swap(outgoing.reshape(peers, chunk, half), ROWS).reshape(peers * chunk, half)

    gathered = plane
    for bit in bits[::-1]:
        gathered = jnp.concatenate([gathered, flip(gathered, "x", bit)], axis=0)

    def x_index(x):
        apart = x ^ x_here
        index = jnp.zeros_like(apart)
        for bit in bits:
            index = index * 2 + (apart // bit) % 2
        return index

    a = jnp.arange(own, dtype=jnp.int32)
    i_of, z_of, top = a % share, a // share % nz, a // (share * nz)
    slot = jnp.arange(2 * own, dtype=jnp.int32)
    picked = []
    for c in range(nc):
        side = nx // nc
        for_qkv = (x_index(top) * nz + z_of) * 2 + c
        for_proj = (x_index(c * side + top % side) * nz + z_of) * 2 + top // side
        place = jnp.where(rep == 3, for_proj, for_qkv) * share + i_of
        picked.append(mm((place[:, None] == slot[None, :]).astype(bf), gathered, NN, bf))
    kept = jnp.where(core == 0, picked[0], picked[1])
    theirs = lax.ppermute(jnp.where(core == 0, picked[1], picked[0]), "core", pair)
    parts = jnp.concatenate([kept, theirs], axis=0)
    weights = [parts] + [shift(parts, "rep", k) for k in range(1, nr)]

    def order(count):
        nat = jnp.arange(count, dtype=jnp.int32)
        i, c, z, x = nat % share, nat // share % nc, nat // (share * nc) % nz, nat // (share * nc * nz)
        pos = c * (count // nc) + (x * nz + z) * share + i
        return (pos[:, None] == nat[None, :]).astype(bf)

    perm = order(channels)
    own_perm = order(own)
    other_feat = lax.ppermute(feature, "core", pair)
    x_pair = mm(jnp.concatenate([feature, other_feat], axis=0), perm, NN, bf)
    grad_hil = jnp.concatenate([mm(recv[h], arrived, TN, bf) for h in range(2)], axis=1)
    other_grad = lax.ppermute(grad_hil, "core", pair)
    place = jnp.stack([core, rep])
    p_own, p_other, term = patch_step(place, x_pair, weights, grad_hil, other_grad, own_perm, nx)

    near = swap(term.reshape(nx * nc * nr, own // nx, own), ("x", "core", "rep"))
    near = jnp.sum(near.reshape(nx, nc, nr, nz, share, own).astype(f32), axis=(0, 2)).astype(bf)
    total = jnp.swapaxes(near, 0, 1).reshape(nz, nc * share, own)

    from_other = lax.ppermute(p_other, "core", pair)
    grad_hfeat = (p_own + from_other.astype(f32)).astype(bf)
    going = (mm(recv[0], grad_hfeat[:, :half], NN) + mm(recv[1], grad_hfeat[:, half:], NN)).astype(bf)
    total, going = lax.optimization_barrier((total, going))
    returned = swap(going.reshape(peers, chunk, half), ROWS)

    for axis, here in (("zl", lax.axis_index("zl")), ("zh", lax.axis_index("zh"))):
        size = lax.axis_size(axis)
        bit = 1
        while bit < size:
            blocks = total.reshape(total.shape[0] // 2, 2, nc * share, own)
            odd = here // bit % 2 == 1
            stay = jnp.where(odd, blocks[:, 1], blocks[:, 0])
            come = flip(jnp.where(odd, blocks[:, 0], blocks[:, 1]), axis, bit)
            total = stay.astype(f32) + come.astype(f32)
            total = total if total.shape[0] == 1 else total.astype(bf)
            bit *= 2
    total, returned = lax.optimization_barrier((total[0], returned))
    returned = returned.reshape(peers * chunk, half)
    last = swap(jnp.broadcast_to(total[None], (nx * nr, nc * share, own)), ("x", "rep"))
    last = last.reshape(nx, nr, nc, share, own)
    here = lax.dynamic_index_in_dim(last, x_here, 0, keepdims=False)
    partner = lax.dynamic_index_in_dim(last, (x_here + nx // 2) % nx, 0, keepdims=False)
    cols = [here[p, c] for p in range(3) for c in range(nc)]
    proj_cols = [lax.dynamic_index_in_dim(m[3], x_here // (nx // nc), 0, keepdims=False) for m in (here, partner)]
    grad_perm = jnp.concatenate([mm(send[h], returned, TN, bf) for h in range(2)], axis=1)
    grad_z = mm(grad_perm, perm, NT, bf)
    return (grad_z[None], jnp.concatenate(cols, axis=1), jnp.concatenate(proj_cols, axis=1))


def solution(mesh):
    rows, reps = mesh.devices.shape
    fine = Mesh(
        mesh.devices.reshape(rows // (Z_HIGH * Z_LOW * CORES), Z_HIGH, Z_LOW, CORES, reps),
        ROWS + ("rep",),
    )
    placed = (
        P("rep", ROWS, None),
        P("rep", ROWS, None),
        P(ROWS, None),
        P(ROWS, None),
        P("rep", ROWS),
        P("rep", ROWS),
    )
    return jax.shard_map(
        per_device,
        mesh=fine,
        in_specs=placed,
        out_specs=(P("rep", ROWS, None), P(ROWS, None), P(ROWS, None)),
        check_vma=False,
    )
```

```python
import jax
import jax.numpy as jnp
from jax import lax
from jax.experimental import pallas as pl
from jax.experimental.pallas import tpu as pltpu
from jax.sharding import Mesh
from jax.sharding import PartitionSpec as P

HEADS = 8
CAP = 2
BLK = 2
Z_HIGH = 4
Z_LOW = 4
CORES = 2
ROWS = ("x", "zh", "zl", "core")
INTERPRET = False
NN = ((1,), (0,))
NT = ((1,), (1,))
TN = ((0,), (0,))


def mm(left, right, dims, out=jnp.float32):
    res = lax.dot_general(left, right, (dims, ((), ())), preferred_element_type=jnp.float32)
    return res.astype(out)


def rank_within(order_keys, owners):
    same_owner = owners[None, :] == owners[:, None]
    earlier = order_keys[None, :] < order_keys[:, None]
    return jnp.sum(jnp.logical_and(same_owner, earlier).astype(jnp.int32), axis=1)


def slot_tables(owners, ranks, count):
    base = owners * (2 * CAP * BLK) + ranks * BLK
    rows = (base[:, None] + jnp.arange(BLK, dtype=jnp.int32)[None, :]).reshape(-1)
    slots = jnp.arange(count * 2 * CAP * BLK, dtype=jnp.int32)
    return [
        (slots[:, None] == (rows + half * CAP * BLK)[None, :]).astype(jnp.bfloat16)
        for half in range(2)
    ]


def swap(block, axis):
    return lax.all_to_all(block, axis, split_axis=0, concat_axis=0, tiled=True)


def shift(block, axis, step):
    count = lax.axis_size(axis)
    return lax.ppermute(block, axis, [(here, (here + step) % count) for here in range(count)])


def flip(block, axis, bit):
    count = lax.axis_size(axis)
    return lax.ppermute(block, axis, [(here, here ^ bit) for here in range(count)])


def attend(qkv, grad_attn, own, head_size):
    bf = jnp.bfloat16
    rows = qkv.shape[0]
    scale = head_size ** (-0.5)
    query, key, value = qkv[:, :own], qkv[:, own : 2 * own], qkv[:, 2 * own :]
    key_t, value_t = key.T, value.T
    two = 2 * head_size
    first = lax.broadcasted_iota(jnp.int32, (rows, two), 1) < head_size
    attn_t, dq_t, dk, dv = [], [], [], []
    for pair in range(own // two):
        cols = slice(pair * two, (pair + 1) * two)
        q_pair, k_pair, v_pair, g_pair = query[:, cols], key[:, cols], value[:, cols], grad_attn[:, cols]
        zero = jnp.zeros_like(k_pair)
        dk_pair, dv_pair = [], []
        for member in range(2):
            k_head = jnp.where(first, k_pair, zero) if member == 0 else jnp.where(first, zero, k_pair)
            v_head = jnp.where(first, v_pair, zero) if member == 0 else jnp.where(first, zero, v_pair)
            score = mm(k_head, q_pair, NT)
            raised = jnp.exp((score - jnp.max(score, axis=0, keepdims=True)) * scale)
            probs = raised * (1.0 / jnp.sum(raised, axis=0, keepdims=True))
            probs_b = probs.astype(bf)
            dprob = mm(v_head, g_pair, NT)
            delta = jnp.sum(probs * dprob, axis=0, keepdims=True)
            dscore = (probs * (dprob - delta) * scale).astype(bf)
            lo = pair * two + member * head_size
            attn_t.append(mm(value_t[lo : lo + head_size], probs_b, NN, bf))
            dq_t.append(mm(key_t[lo : lo + head_size], dscore, NN, bf))
            dk_pair.append(mm(dscore, q_pair, NN))
            dv_pair.append(mm(probs_b, g_pair, NN))
        dk.append(jnp.where(first, dk_pair[0], dk_pair[1]).astype(bf))
        dv.append(jnp.where(first, dv_pair[0], dv_pair[1]).astype(bf))
    grad_q = jnp.concatenate(dq_t, axis=0).T
    return jnp.concatenate(attn_t, axis=0), jnp.concatenate([grad_q] + dk + dv, axis=1)


def patch_body(
    place_ref, x_ref, w0_ref, w1_ref, w2_ref, w3_ref, gown_ref, goth_ref, own_perm_ref,
    pown_ref, poth_ref, keep_ref, send_ref, w_ref, tq_ref, tp_ref,
):
    bf = jnp.bfloat16
    core, rep = place_ref[0], place_ref[1]
    channels = x_ref.shape[1]
    own = channels // CORES
    rows = gown_ref.shape[0]
    part = own // CORES
    for k, ref in enumerate((w0_ref, w1_ref, w2_ref, w3_ref)):
        slot = lax.rem(rep + 4 - k, 4)
        w_ref[slot, core] = ref[:own]
        w_ref[slot, 1 - core] = ref[own:]
    w_qkv = jnp.concatenate([w_ref[p].reshape(channels, own) for p in range(3)], axis=1)
    cols = [
        jnp.concatenate([w_ref[3, c, h * part : (h + 1) * part] for c in range(CORES)], axis=0) for h in range(2)
    ]
    own_perm = own_perm_ref[...]
    w_proj = mm(own_perm, jnp.concatenate(cols, axis=1), NN, bf)
    x = x_ref[...]
    grad_pair = jnp.concatenate([gown_ref[...], goth_ref[...]], axis=0)
    qkv = mm(x, w_qkv, NN, bf)
    grad_attn = mm(grad_pair, w_proj, NT, bf)
    attn_t, grad_qkv = attend(qkv, grad_attn, own, channels // HEADS)
    tq_ref[...] = mm(x, grad_qkv, TN, bf).reshape(CORES, own, 3 * own)
    proj_term = mm(attn_t, grad_pair, NN, bf)
    tp_ref[...] = mm(own_perm, proj_term, TN, bf).reshape(CORES, part, channels)
    for out_ref, side in ((keep_ref, core), (send_ref, 1 - core)):
        out_ref[:, : 3 * own] = tq_ref[side]
        out_ref[:part, 3 * own :] = tp_ref[side, :, :own]
        out_ref[part:, 3 * own :] = tp_ref[side, :, own:]
    partial = mm(grad_qkv, w_qkv, NT)
    pown_ref[...] = partial[:rows]
    poth_ref[...] = partial[rows:].astype(bf)


def patch_step(place, x, weights, gown, goth, own_perm):
    bf = jnp.bfloat16
    rows, channels = gown.shape
    own = channels // CORES
    vmem = pl.BlockSpec(memory_space=pltpu.VMEM)
    return pl.pallas_call(
        patch_body,
        out_shape=[
            jax.ShapeDtypeStruct((rows, channels), jnp.float32),
            jax.ShapeDtypeStruct((rows, channels), bf),
            jax.ShapeDtypeStruct((own, 4 * own), bf),
            jax.ShapeDtypeStruct((own, 4 * own), bf),
        ],
        in_specs=[pl.BlockSpec(memory_space=pltpu.SMEM)] + [vmem] * 8,
        out_specs=[vmem] * 4,
        scratch_shapes=[
            pltpu.VMEM((4, CORES, own, own), bf),
            pltpu.VMEM((CORES, own, 3 * own), bf),
            pltpu.VMEM((CORES, own // CORES, channels), bf),
        ],
        compiler_params=pltpu.CompilerParams(vmem_limit_bytes=48 << 20),
        interpret=INTERPRET,
    )(place, x, *weights, gown, goth, own_perm)


def per_device(feats, grad_out, qkv_weight, proj_weight, to_hilbert, to_zorder):
    bf = jnp.bfloat16
    f32 = jnp.float32
    nx, zh, zl, nc, nr = (lax.axis_size(a) for a in ROWS + ("rep",))
    nz = zh * zl
    peers = nx * nz * nc
    x_here, core, rep = (lax.axis_index(a) for a in ("x", "core", "rep"))
    feature = feats[0]
    rows_dev, channels = feature.shape
    own = channels // nc
    part = own // nc
    half = channels // 2
    share = qkv_weight.shape[0]
    blocks_dev = to_hilbert.shape[1]
    chunk = 2 * CAP * BLK
    pair = [(0, 1), (1, 0)]
    bits = [1 << b for b in range(nx.bit_length() - 1)]

    mine = lax.dynamic_slice_in_dim(jnp.concatenate([qkv_weight, proj_weight], axis=1), rep * channels, channels, 1)
    mine = jnp.concatenate([mine[:, :own], mine[:, own:]], axis=0)
    plane = swap(jnp.broadcast_to(mine[None], (nz, 2 * share, own)), ("zh", "zl")).reshape(nz * 2 * share, own)

    ids = jnp.arange(blocks_dev, dtype=jnp.int32)
    target = to_hilbert[0] // blocks_dev
    send = slot_tables(target, rank_within(ids, target), peers)
    source = to_zorder[0] // blocks_dev
    recv = slot_tables(source, rank_within(to_zorder[0], source), peers)
    grad_z_in = grad_out[0]
    outgoing = (mm(send[0], grad_z_in[:, :half], NN) + mm(send[1], grad_z_in[:, half:], NN)).astype(bf)
    outgoing, plane = lax.optimization_barrier((outgoing, plane))
    arrived = swap(outgoing.reshape(peers, chunk, half), ROWS).reshape(peers * chunk, half)

    gathered = plane
    for bit in bits[::-1]:
        gathered = jnp.concatenate([gathered, flip(gathered, "x", bit)], axis=0)

    def x_index(x):
        apart = x ^ x_here
        index = jnp.zeros_like(apart)
        for bit in bits:
            index = index * 2 + (apart // bit) % 2
        return index

    a = jnp.arange(own, dtype=jnp.int32)
    i_of, z_of, top = a % share, a // share % nz, a // (share * nz)
    slot = jnp.arange(2 * own, dtype=jnp.int32)
    picked = []
    for c in range(nc):
        side = nx // nc
        for_qkv = (x_index(top) * nz + z_of) * 2 + c
        for_proj = (x_index(c * side + top % side) * nz + z_of) * 2 + top // side
        place = jnp.where(rep == 3, for_proj, for_qkv) * share + i_of
        picked.append(mm((place[:, None] == slot[None, :]).astype(bf), gathered, NN, bf))
    kept = jnp.where(core == 0, picked[0], picked[1])
    theirs = lax.ppermute(jnp.where(core == 0, picked[1], picked[0]), "core", pair)
    parts = jnp.concatenate([kept, theirs], axis=0)
    weights = [parts] + [shift(parts, "rep", k) for k in range(1, nr)]

    def order(count):
        nat = jnp.arange(count, dtype=jnp.int32)
        i, c, z, x = nat % share, nat // share % nc, nat // (share * nc) % nz, nat // (share * nc * nz)
        pos = c * (count // nc) + (x * nz + z) * share + i
        return (pos[:, None] == nat[None, :]).astype(bf)

    perm = order(channels)
    own_perm = order(own)
    other_feat = lax.ppermute(feature, "core", pair)
    x_pair = mm(jnp.concatenate([feature, other_feat], axis=0), perm, NN, bf)
    grad_hil = jnp.concatenate([mm(recv[h], arrived, TN, bf) for h in range(2)], axis=1)
    other_grad = lax.ppermute(grad_hil, "core", pair)
    place = jnp.stack([core, rep])
    p_own, p_other, keep, away = patch_step(place, x_pair, weights, grad_hil, other_grad, own_perm)

    from_other = lax.ppermute(p_other, "core", pair)
    grad_hfeat = (p_own + from_other.astype(f32)).astype(bf)
    going = (mm(recv[0], grad_hfeat[:, :half], NN) + mm(recv[1], grad_hfeat[:, half:], NN)).astype(bf)
    returned = swap(going.reshape(peers, chunk, half), ROWS).reshape(peers * chunk, half)

    got = lax.ppermute(away, "core", pair)
    proj = [jnp.concatenate([m[:part, 3 * own :], m[part:, 3 * own :]], axis=1) for m in (keep, got)]
    proj = jnp.concatenate([jnp.where(core == 0, proj[0], proj[1]), jnp.where(core == 0, proj[1], proj[0])], axis=0)
    total = jnp.concatenate([keep[:, : 3 * own], got[:, : 3 * own], proj], axis=1)

    def halve(value, axis, here, bit, first, second):
        mine_set = here // bit % 2 == 1
        stay = jnp.where(mine_set, second, first)
        come = flip(jnp.where(mine_set, first, second), axis, bit)
        return (stay.astype(f32) + come.astype(f32)).astype(bf)

    wide = total.shape[1] // 2
    total = halve(total, "rep", rep, 1, total[:, :wide], total[:, wide:])
    for bit in bits:
        count = nx // bit
        blocks = total.reshape(count // 2, 2, nz * share, total.shape[1])
        flat = (count // 2 * nz * share, total.shape[1])
        total = halve(total, "x", x_here, bit, blocks[:, 0].reshape(flat), blocks[:, 1].reshape(flat))
    total, returned = lax.optimization_barrier((total, returned))
    far = swap(total.reshape(nz, share, wide), ("zh", "zl"))
    summed = jnp.sum(far.astype(f32), axis=0)
    last = swap(jnp.broadcast_to(summed[None], (nr, share, wide)), "rep")
    last = jnp.concatenate([last[0] + last[2], last[1] + last[3]], axis=1)
    grad_perm = jnp.concatenate([mm(send[h], returned, TN, bf) for h in range(2)], axis=1)
    grad_z = mm(grad_perm, perm, NT, bf)
    lower = jnp.where(core == 0, last[:, : 3 * own], last[:, 3 * own : 6 * own])
    upper = jnp.where(core == 0, last[:, 3 * own : 6 * own], last[:, : 3 * own])
    cols = []
    for p in range(3):
        cols += [lower[:, p * own : (p + 1) * own], upper[:, p * own : (p + 1) * own]]
    return (grad_z[None], jnp.concatenate(cols, axis=1), last[:, 6 * own :])


def solution(mesh):
    rows, reps = mesh.devices.shape
    fine = Mesh(
        mesh.devices.reshape(rows // (Z_HIGH * Z_LOW * CORES), Z_HIGH, Z_LOW, CORES, reps),
        ROWS + ("rep",),
    )
    placed = (
        P("rep", ROWS, None),
        P("rep", ROWS, None),
        P(ROWS, None),
        P(ROWS, None),
        P("rep", ROWS),
        P("rep", ROWS),
    )
    return jax.shard_map(
        per_device,
        mesh=fine,
        in_specs=placed,
        out_specs=(P("rep", ROWS, None), P(ROWS, None), P(ROWS, None)),
        check_vma=False,
    )
```

```python
import jax
import jax.numpy as jnp
from jax import lax
from jax.experimental import pallas as pl
from jax.experimental.pallas import tpu as pltpu
from jax.sharding import Mesh
from jax.sharding import PartitionSpec as P

HEADS = 8
CAP = 2
BLK = 2
Z_HIGH = 4
Z_LOW = 4
CORES = 2
ROWS = ("x", "zh", "zl", "core")
INTERPRET = False
NN = ((1,), (0,))
NT = ((1,), (1,))
TN = ((0,), (0,))


def mm(left, right, dims, out=jnp.float32):
    res = lax.dot_general(left, right, (dims, ((), ())), preferred_element_type=jnp.float32)
    return res.astype(out)


def rank_within(order_keys, owners):
    same_owner = owners[None, :] == owners[:, None]
    earlier = order_keys[None, :] < order_keys[:, None]
    return jnp.sum(jnp.logical_and(same_owner, earlier).astype(jnp.int32), axis=1)


def slot_tables(owners, ranks, count):
    base = owners * (2 * CAP * BLK) + ranks * BLK
    rows = (base[:, None] + jnp.arange(BLK, dtype=jnp.int32)[None, :]).reshape(-1)
    slots = jnp.arange(count * 2 * CAP * BLK, dtype=jnp.int32)
    return [
        (slots[:, None] == (rows + half * CAP * BLK)[None, :]).astype(jnp.bfloat16)
        for half in range(2)
    ]


def swap(block, axis):
    return lax.all_to_all(block, axis, split_axis=0, concat_axis=0, tiled=True)


def shift(block, axis, step):
    count = lax.axis_size(axis)
    return lax.ppermute(block, axis, [(here, (here + step) % count) for here in range(count)])


def flip(block, axis, bit):
    count = lax.axis_size(axis)
    return lax.ppermute(block, axis, [(here, here ^ bit) for here in range(count)])


def attend(qkv, grad_attn, own, head_size):
    bf = jnp.bfloat16
    rows = qkv.shape[0]
    scale = head_size ** (-0.5)
    query, key, value = qkv[:, :own], qkv[:, own : 2 * own], qkv[:, 2 * own :]
    key_t, value_t = key.T, value.T
    two = 2 * head_size
    first = lax.broadcasted_iota(jnp.int32, (rows, two), 1) < head_size
    attn_t, dq_t, dk, dv = [], [], [], []
    for pair in range(own // two):
        cols = slice(pair * two, (pair + 1) * two)
        q_pair, k_pair, v_pair, g_pair = query[:, cols], key[:, cols], value[:, cols], grad_attn[:, cols]
        zero = jnp.zeros_like(k_pair)
        dk_pair, dv_pair = [], []
        for member in range(2):
            k_head = jnp.where(first, k_pair, zero) if member == 0 else jnp.where(first, zero, k_pair)
            v_head = jnp.where(first, v_pair, zero) if member == 0 else jnp.where(first, zero, v_pair)
            score = mm(k_head, q_pair, NT)
            raised = jnp.exp((score - jnp.max(score, axis=0, keepdims=True)) * scale)
            probs = raised * (1.0 / jnp.sum(raised, axis=0, keepdims=True))
            probs_b = probs.astype(bf)
            dprob = mm(v_head, g_pair, NT)
            delta = jnp.sum(probs * dprob, axis=0, keepdims=True)
            dscore = (probs * (dprob - delta) * scale).astype(bf)
            lo = pair * two + member * head_size
            attn_t.append(mm(value_t[lo : lo + head_size], probs_b, NN, bf))
            dq_t.append(mm(key_t[lo : lo + head_size], dscore, NN, bf))
            dk_pair.append(mm(dscore, q_pair, NN))
            dv_pair.append(mm(probs_b, g_pair, NN))
        dk.append(jnp.where(first, dk_pair[0], dk_pair[1]).astype(bf))
        dv.append(jnp.where(first, dv_pair[0], dv_pair[1]).astype(bf))
    grad_q = jnp.concatenate(dq_t, axis=0).T
    return jnp.concatenate(attn_t, axis=0), jnp.concatenate([grad_q] + dk + dv, axis=1)


def patch_body(
    place_ref, x_ref, w0_ref, w1_ref, w2_ref, w3_ref, gown_ref, goth_ref, own_perm_ref,
    pown_ref, poth_ref, keep_ref, send_ref, w_ref, tq_ref, tp_ref,
):
    bf = jnp.bfloat16
    core, rep = place_ref[0], place_ref[1]
    channels = x_ref.shape[1]
    own = channels // CORES
    rows = gown_ref.shape[0]
    part = own // CORES
    for k, ref in enumerate((w0_ref, w1_ref, w2_ref, w3_ref)):
        slot = lax.rem(rep + 4 - k, 4)
        w_ref[slot, core] = ref[:own]
        w_ref[slot, 1 - core] = ref[own:]
    w_qkv = jnp.concatenate([w_ref[p].reshape(channels, own) for p in range(3)], axis=1)
    cols = [
        jnp.concatenate([w_ref[3, c, h * part : (h + 1) * part] for c in range(CORES)], axis=0) for h in range(2)
    ]
    own_perm = own_perm_ref[...]
    w_proj = mm(own_perm, jnp.concatenate(cols, axis=1), NN, bf)
    x = x_ref[...]
    grad_pair = jnp.concatenate([gown_ref[...], goth_ref[...]], axis=0)
    qkv = mm(x, w_qkv, NN, bf)
    grad_attn = mm(grad_pair, w_proj, NT, bf)
    attn_t, grad_qkv = attend(qkv, grad_attn, own, channels // HEADS)
    tq_ref[...] = mm(x, grad_qkv, TN, bf).reshape(CORES, own, 3 * own)
    proj_term = mm(attn_t, grad_pair, NN, bf)
    tp_ref[...] = mm(own_perm, proj_term, TN, bf).reshape(CORES, part, channels)
    for out_ref, side in ((keep_ref, core), (send_ref, 1 - core)):
        out_ref[:, : 3 * own] = tq_ref[side]
        out_ref[:part, 3 * own :] = tp_ref[side, :, :own]
        out_ref[part:, 3 * own :] = tp_ref[side, :, own:]
    partial = mm(grad_qkv, w_qkv, NT)
    pown_ref[...] = partial[:rows]
    poth_ref[...] = partial[rows:].astype(bf)


def patch_step(place, x, weights, gown, goth, own_perm):
    bf = jnp.bfloat16
    rows, channels = gown.shape
    own = channels // CORES
    vmem = pl.BlockSpec(memory_space=pltpu.VMEM)
    return pl.pallas_call(
        patch_body,
        out_shape=[
            jax.ShapeDtypeStruct((rows, channels), jnp.float32),
            jax.ShapeDtypeStruct((rows, channels), bf),
            jax.ShapeDtypeStruct((own, 4 * own), bf),
            jax.ShapeDtypeStruct((own, 4 * own), bf),
        ],
        in_specs=[pl.BlockSpec(memory_space=pltpu.SMEM)] + [vmem] * 8,
        out_specs=[vmem] * 4,
        scratch_shapes=[
            pltpu.VMEM((4, CORES, own, own), bf),
            pltpu.VMEM((CORES, own, 3 * own), bf),
            pltpu.VMEM((CORES, own // CORES, channels), bf),
        ],
        compiler_params=pltpu.CompilerParams(vmem_limit_bytes=48 << 20),
        interpret=INTERPRET,
    )(place, x, *weights, gown, goth, own_perm)


def per_device(feats, grad_out, qkv_weight, proj_weight, to_hilbert, to_zorder):
    bf = jnp.bfloat16
    f32 = jnp.float32
    nx, zh, zl, nc, nr = (lax.axis_size(a) for a in ROWS + ("rep",))
    nz = zh * zl
    peers = nx * nz * nc
    x_here, core, rep = (lax.axis_index(a) for a in ("x", "core", "rep"))
    feature = feats[0]
    rows_dev, channels = feature.shape
    own = channels // nc
    part = own // nc
    half = channels // 2
    share = qkv_weight.shape[0]
    blocks_dev = to_hilbert.shape[1]
    chunk = 2 * CAP * BLK
    pair = [(0, 1), (1, 0)]
    bits = [1 << b for b in range(nx.bit_length() - 1)]

    mine = lax.dynamic_slice_in_dim(jnp.concatenate([qkv_weight, proj_weight], axis=1), rep * channels, channels, 1)
    mine = jnp.concatenate([mine[:, :own], mine[:, own:]], axis=0)
    plane = swap(jnp.broadcast_to(mine[None], (nz, 2 * share, own)), ("zh", "zl")).reshape(nz * 2 * share, own)

    ids = jnp.arange(blocks_dev, dtype=jnp.int32)
    target = to_hilbert[0] // blocks_dev
    send = slot_tables(target, rank_within(ids, target), peers)
    source = to_zorder[0] // blocks_dev
    recv = slot_tables(source, rank_within(to_zorder[0], source), peers)
    grad_z_in = grad_out[0]
    outgoing = (mm(send[0], grad_z_in[:, :half], NN) + mm(send[1], grad_z_in[:, half:], NN)).astype(bf)
    outgoing, plane = lax.optimization_barrier((outgoing, plane))
    arrived = swap(outgoing.reshape(peers, chunk, half), ROWS).reshape(peers * chunk, half)

    gathered = plane
    for bit in bits[::-1]:
        gathered = jnp.concatenate([gathered, flip(gathered, "x", bit)], axis=0)

    def x_index(x):
        apart = x ^ x_here
        index = jnp.zeros_like(apart)
        for bit in bits:
            index = index * 2 + (apart // bit) % 2
        return index

    a = jnp.arange(own, dtype=jnp.int32)
    i_of, z_of, top = a % share, a // share % nz, a // (share * nz)
    slot = jnp.arange(2 * own, dtype=jnp.int32)
    picked = []
    for c in range(nc):
        side = nx // nc
        for_qkv = (x_index(top) * nz + z_of) * 2 + c
        for_proj = (x_index(c * side + top % side) * nz + z_of) * 2 + top // side
        place = jnp.where(rep == 3, for_proj, for_qkv) * share + i_of
        picked.append(mm((place[:, None] == slot[None, :]).astype(bf), gathered, NN, bf))
    kept = jnp.where(core == 0, picked[0], picked[1])
    theirs = lax.ppermute(jnp.where(core == 0, picked[1], picked[0]), "core", pair)
    parts = jnp.concatenate([kept, theirs], axis=0)
    weights = [parts] + [shift(parts, "rep", k) for k in range(1, nr)]

    def order(count):
        nat = jnp.arange(count, dtype=jnp.int32)
        i, c, z, x = nat % share, nat // share % nc, nat // (share * nc) % nz, nat // (share * nc * nz)
        pos = c * (count // nc) + (x * nz + z) * share + i
        return (pos[:, None] == nat[None, :]).astype(bf)

    perm = order(channels)
    own_perm = order(own)
    other_feat = lax.ppermute(feature, "core", pair)
    x_pair = mm(jnp.concatenate([feature, other_feat], axis=0), perm, NN, bf)
    grad_hil = jnp.concatenate([mm(recv[h], arrived, TN, bf) for h in range(2)], axis=1)
    other_grad = lax.ppermute(grad_hil, "core", pair)
    place = jnp.stack([core, rep])
    p_own, p_other, keep, away = patch_step(place, x_pair, weights, grad_hil, other_grad, own_perm)

    from_other = lax.ppermute(p_other, "core", pair)
    grad_hfeat = (p_own + from_other.astype(f32)).astype(bf)
    going = (mm(recv[0], grad_hfeat[:, :half], NN) + mm(recv[1], grad_hfeat[:, half:], NN)).astype(bf)
    returned = swap(going.reshape(peers, chunk, half), ROWS).reshape(peers * chunk, half)

    got = lax.ppermute(away, "core", pair)
    proj = [jnp.concatenate([m[:part, 3 * own :], m[part:, 3 * own :]], axis=1) for m in (keep, got)]
    proj = jnp.concatenate([jnp.where(core == 0, proj[0], proj[1]), jnp.where(core == 0, proj[1], proj[0])], axis=0)
    total = jnp.concatenate([keep[:, : 3 * own], got[:, : 3 * own], proj], axis=1)

    def halve(value, axis, here, bit, first, second):
        mine_set = here // bit % 2 == 1
        stay = jnp.where(mine_set, second, first)
        come = flip(jnp.where(mine_set, first, second), axis, bit)
        return (stay.astype(f32) + come.astype(f32)).astype(bf)

    def over_x(value, bit):
        count = nx // bit
        blocks = value.reshape(count // 2, 2, nz * share, value.shape[1])
        flat = (count // 2 * nz * share, value.shape[1])
        return halve(value, "x", x_here, bit, blocks[:, 0].reshape(flat), blocks[:, 1].reshape(flat))

    def over_rep(value):
        wide = value.shape[1] // 2
        return halve(value, "rep", rep, 1, value[:, :wide], value[:, wide:])

    wide = total.shape[1] // 2
    left, right = total[:, :wide], total[:, wide:]
    left = over_x(over_rep(left), 1)
    right = over_rep(over_x(right, 1))
    for bit in bits[1:]:
        left, right = over_x(left, bit), over_x(right, bit)
    total = jnp.concatenate([left, right], axis=1)
    total, returned = lax.optimization_barrier((total, returned))
    far = swap(total.reshape(nz, share, wide), ("zh", "zl"))
    summed = jnp.sum(far.astype(f32), axis=0)
    last = swap(jnp.broadcast_to(summed[None], (nr, share, wide)), "rep")
    last = jnp.concatenate([last[k, :, s] + last[k + 2, :, s] for s in (slice(None, wide // 2), slice(wide // 2, None)) for k in range(2)], axis=1)
    grad_perm = jnp.concatenate([mm(send[h], returned, TN, bf) for h in range(2)], axis=1)
    grad_z = mm(grad_perm, perm, NT, bf)
    lower = jnp.where(core == 0, last[:, : 3 * own], last[:, 3 * own : 6 * own])
    upper = jnp.where(core == 0, last[:, 3 * own : 6 * own], last[:, : 3 * own])
    cols = []
    for p in range(3):
        cols += [lower[:, p * own : (p + 1) * own], upper[:, p * own : (p + 1) * own]]
    return (grad_z[None], jnp.concatenate(cols, axis=1), last[:, 6 * own :])


def solution(mesh):
    rows, reps = mesh.devices.shape
    fine = Mesh(
        mesh.devices.reshape(rows // (Z_HIGH * Z_LOW * CORES), Z_HIGH, Z_LOW, CORES, reps),
        ROWS + ("rep",),
    )
    placed = (
        P("rep", ROWS, None),
        P("rep", ROWS, None),
        P(ROWS, None),
        P(ROWS, None),
        P("rep", ROWS),
        P("rep", ROWS),
    )
    return jax.shard_map(
        per_device,
        mesh=fine,
        in_specs=placed,
        out_specs=(P("rep", ROWS, None), P(ROWS, None), P(ROWS, None)),
        check_vma=False,
    )
```

```python
import jax
import jax.numpy as jnp
from jax import lax
from jax.experimental import pallas as pl
from jax.experimental.pallas import tpu as pltpu
from jax.sharding import Mesh
from jax.sharding import PartitionSpec as P

HEADS = 8
CAP = 2
BLK = 2
Z_HIGH = 4
Z_LOW = 4
CORES = 2
ROWS = ("x", "zh", "zl", "core")
INTERPRET = False
NN = ((1,), (0,))
NT = ((1,), (1,))
TN = ((0,), (0,))


def mm(left, right, dims, out=jnp.float32):
    res = lax.dot_general(left, right, (dims, ((), ())), preferred_element_type=jnp.float32)
    return res.astype(out)


def rank_within(order_keys, owners):
    same_owner = owners[None, :] == owners[:, None]
    earlier = order_keys[None, :] < order_keys[:, None]
    return jnp.sum(jnp.logical_and(same_owner, earlier).astype(jnp.int32), axis=1)


def slot_tables(owners, ranks, count):
    base = owners * (2 * CAP * BLK) + ranks * BLK
    rows = (base[:, None] + jnp.arange(BLK, dtype=jnp.int32)[None, :]).reshape(-1)
    slots = jnp.arange(count * 2 * CAP * BLK, dtype=jnp.int32)
    return [
        (slots[:, None] == (rows + half * CAP * BLK)[None, :]).astype(jnp.bfloat16)
        for half in range(2)
    ]


def swap(block, axis):
    return lax.all_to_all(block, axis, split_axis=0, concat_axis=0, tiled=True)


def shift(block, axis, step):
    count = lax.axis_size(axis)
    return lax.ppermute(block, axis, [(here, (here + step) % count) for here in range(count)])


def flip(block, axis, bit):
    count = lax.axis_size(axis)
    return lax.ppermute(block, axis, [(here, here ^ bit) for here in range(count)])


def attend(qkv, grad_attn, own, head_size):
    bf = jnp.bfloat16
    rows = qkv.shape[0]
    scale = head_size ** (-0.5)
    query, key, value = qkv[:, :own], qkv[:, own : 2 * own], qkv[:, 2 * own :]
    key_t, value_t = key.T, value.T
    two = 2 * head_size
    first = lax.broadcasted_iota(jnp.int32, (rows, two), 1) < head_size
    attn_t, dq_t, dk, dv = [], [], [], []
    for pair in range(own // two):
        cols = slice(pair * two, (pair + 1) * two)
        q_pair, k_pair, v_pair, g_pair = query[:, cols], key[:, cols], value[:, cols], grad_attn[:, cols]
        zero = jnp.zeros_like(k_pair)
        dk_pair, dv_pair = [], []
        for member in range(2):
            k_head = jnp.where(first, k_pair, zero) if member == 0 else jnp.where(first, zero, k_pair)
            v_head = jnp.where(first, v_pair, zero) if member == 0 else jnp.where(first, zero, v_pair)
            score = mm(k_head, q_pair, NT)
            raised = jnp.exp((score - jnp.max(score, axis=0, keepdims=True)) * scale)
            probs = raised * (1.0 / jnp.sum(raised, axis=0, keepdims=True))
            probs_b = probs.astype(bf)
            dprob = mm(v_head, g_pair, NT)
            delta = jnp.sum(probs * dprob, axis=0, keepdims=True)
            dscore = (probs * (dprob - delta) * scale).astype(bf)
            lo = pair * two + member * head_size
            attn_t.append(mm(value_t[lo : lo + head_size], probs_b, NN, bf))
            dq_t.append(mm(key_t[lo : lo + head_size], dscore, NN, bf))
            dk_pair.append(mm(dscore, q_pair, NN))
            dv_pair.append(mm(probs_b, g_pair, NN))
        dk.append(jnp.where(first, dk_pair[0], dk_pair[1]).astype(bf))
        dv.append(jnp.where(first, dv_pair[0], dv_pair[1]).astype(bf))
    grad_q = jnp.concatenate(dq_t, axis=0).T
    return jnp.concatenate(attn_t, axis=0), jnp.concatenate([grad_q] + dk + dv, axis=1)


def patch_body(
    place_ref, x_ref, w0_ref, w1_ref, w2_ref, w3_ref, gown_ref, goth_ref, own_perm_ref,
    pown_ref, poth_ref, term_ref, w_ref,
):
    bf = jnp.bfloat16
    core, rep = place_ref[0], place_ref[1]
    channels = x_ref.shape[1]
    own = channels // CORES
    rows = gown_ref.shape[0]
    part = own // CORES
    for k, ref in enumerate((w0_ref, w1_ref, w2_ref, w3_ref)):
        slot = lax.rem(rep + 4 - k, 4)
        w_ref[slot, core] = ref[:own]
        w_ref[slot, 1 - core] = ref[own:]
    w_qkv = jnp.concatenate([w_ref[p].reshape(channels, own) for p in range(3)], axis=1)
    cols = [
        jnp.concatenate([w_ref[3, c, h * part : (h + 1) * part] for c in range(CORES)], axis=0) for h in range(2)
    ]
    own_perm = own_perm_ref[...]
    w_proj = mm(own_perm, jnp.concatenate(cols, axis=1), NN, bf)
    x = x_ref[...]
    grad_pair = jnp.concatenate([gown_ref[...], goth_ref[...]], axis=0)
    qkv = mm(x, w_qkv, NN, bf)
    grad_attn = mm(grad_pair, w_proj, NT, bf)
    attn_t, grad_qkv = attend(qkv, grad_attn, own, channels // HEADS)
    qkv_term = mm(x, grad_qkv, TN, bf)
    proj_term = mm(own_perm, mm(attn_t, grad_pair, NN, bf), TN, bf)
    nx = term_ref.shape[0]
    tall = own // nx
    for c in range(CORES):
        for there in range(nx):
            lo = c * own + there * tall
            for p in range(3):
                term_ref[there, c, p] = qkv_term[lo : lo + tall, p * own : (p + 1) * own]
            lo = c * part + there % (nx // CORES) * tall
            block = proj_term[lo : lo + tall]
            term_ref[there, c, 3] = jnp.where(core == there // (nx // CORES), block[:, :own], block[:, own:])
    partial = mm(grad_qkv, w_qkv, NT)
    pown_ref[...] = partial[:rows]
    poth_ref[...] = partial[rows:].astype(bf)


def patch_step(place, x, weights, gown, goth, own_perm, nx):
    bf = jnp.bfloat16
    rows, channels = gown.shape
    own = channels // CORES
    vmem = pl.BlockSpec(memory_space=pltpu.VMEM)
    return pl.pallas_call(
        patch_body,
        out_shape=[
            jax.ShapeDtypeStruct((rows, channels), jnp.float32),
            jax.ShapeDtypeStruct((rows, channels), bf),
            jax.ShapeDtypeStruct((nx, CORES, 4, own // nx, own), bf),
        ],
        in_specs=[pl.BlockSpec(memory_space=pltpu.SMEM)] + [vmem] * 8,
        out_specs=[vmem] * 3,
        scratch_shapes=[
            pltpu.VMEM((4, CORES, own, own), bf),
        ],
        compiler_params=pltpu.CompilerParams(vmem_limit_bytes=48 << 20),
        interpret=INTERPRET,
    )(place, x, *weights, gown, goth, own_perm)


def per_device(feats, grad_out, qkv_weight, proj_weight, to_hilbert, to_zorder):
    bf = jnp.bfloat16
    f32 = jnp.float32
    nx, zh, zl, nc, nr = (lax.axis_size(a) for a in ROWS + ("rep",))
    nz = zh * zl
    peers = nx * nz * nc
    x_here, core, rep = (lax.axis_index(a) for a in ("x", "core", "rep"))
    feature = feats[0]
    rows_dev, channels = feature.shape
    own = channels // nc
    part = own // nc
    half = channels // 2
    share = qkv_weight.shape[0]
    blocks_dev = to_hilbert.shape[1]
    chunk = 2 * CAP * BLK
    pair = [(0, 1), (1, 0)]
    bits = [1 << b for b in range(nx.bit_length() - 1)]

    mine = lax.dynamic_slice_in_dim(jnp.concatenate([qkv_weight, proj_weight], axis=1), rep * channels, channels, 1)
    mine = jnp.concatenate([mine[:, :own], mine[:, own:]], axis=0)
    plane = swap(jnp.broadcast_to(mine[None], (nz, 2 * share, own)), ("zh", "zl")).reshape(nz * 2 * share, own)

    ids = jnp.arange(blocks_dev, dtype=jnp.int32)
    target = to_hilbert[0] // blocks_dev
    send = slot_tables(target, rank_within(ids, target), peers)
    source = to_zorder[0] // blocks_dev
    recv = slot_tables(source, rank_within(to_zorder[0], source), peers)
    grad_z_in = grad_out[0]
    outgoing = (mm(send[0], grad_z_in[:, :half], NN) + mm(send[1], grad_z_in[:, half:], NN)).astype(bf)
    outgoing, plane = lax.optimization_barrier((outgoing, plane))
    arrived = swap(outgoing.reshape(peers, chunk, half), ROWS).reshape(peers * chunk, half)

    gathered = plane
    for bit in bits[::-1]:
        gathered = jnp.concatenate([gathered, flip(gathered, "x", bit)], axis=0)

    def x_index(x):
        apart = x ^ x_here
        index = jnp.zeros_like(apart)
        for bit in bits:
            index = index * 2 + (apart // bit) % 2
        return index

    a = jnp.arange(own, dtype=jnp.int32)
    i_of, z_of, top = a % share, a // share % nz, a // (share * nz)
    slot = jnp.arange(2 * own, dtype=jnp.int32)
    picked = []
    for c in range(nc):
        side = nx // nc
        for_qkv = (x_index(top) * nz + z_of) * 2 + c
        for_proj = (x_index(c * side + top % side) * nz + z_of) * 2 + top // side
        place = jnp.where(rep == 3, for_proj, for_qkv) * share + i_of
        picked.append(mm((place[:, None] == slot[None, :]).astype(bf), gathered, NN, bf))
    kept = jnp.where(core == 0, picked[0], picked[1])
    theirs = lax.ppermute(jnp.where(core == 0, picked[1], picked[0]), "core", pair)
    parts = jnp.concatenate([kept, theirs], axis=0)
    weights = [parts] + [shift(parts, "rep", k) for k in range(1, nr)]

    def order(count):
        nat = jnp.arange(count, dtype=jnp.int32)
        i, c, z, x = nat % share, nat // share % nc, nat // (share * nc) % nz, nat // (share * nc * nz)
        pos = c * (count // nc) + (x * nz + z) * share + i
        return (pos[:, None] == nat[None, :]).astype(bf)

    perm = order(channels)
    own_perm = order(own)
    other_feat = lax.ppermute(feature, "core", pair)
    x_pair = mm(jnp.concatenate([feature, other_feat], axis=0), perm, NN, bf)
    grad_hil = jnp.concatenate([mm(recv[h], arrived, TN, bf) for h in range(2)], axis=1)
    other_grad = lax.ppermute(grad_hil, "core", pair)
    place = jnp.stack([core, rep])
    p_own, p_other, term = patch_step(place, x_pair, weights, grad_hil, other_grad, own_perm, nx)

    near = swap(term.reshape(nx * nc * nr, own // nx, own), ("x", "core", "rep"))
    near = jnp.sum(near.reshape(nx, nc, nr, nz, share, own).astype(f32), axis=(0, 2)).astype(bf)
    total = jnp.swapaxes(near, 0, 1).reshape(nz, nc * share, own)

    from_other = lax.ppermute(p_other, "core", pair)
    grad_hfeat = (p_own + from_other.astype(f32)).astype(bf)
    going = (mm(recv[0], grad_hfeat[:, :half], NN) + mm(recv[1], grad_hfeat[:, half:], NN)).astype(bf)
    total = jnp.sum(swap(total, ("zh", "zl")).astype(f32), axis=0)
    total, going = lax.optimization_barrier((total, going))
    returned = swap(going.reshape(peers, chunk, half), ROWS)
    returned = returned.reshape(peers * chunk, half)

    pieces = total.reshape(nc, share, own)
    low = jnp.where(x_here // (nx // nc) == 0, pieces[0], pieces[1])
    high = flip(jnp.where(x_here // (nx // nc) == 0, pieces[1], pieces[0]), "x", nx // 2)
    ready = jnp.where(rep == 3, jnp.stack([low, high]), pieces).reshape(nc * share, own)
    copies = jnp.stack([ready] + [shift(ready, "rep", k) for k in range(1, nr)])
    cols = []
    for p in range(4):
        whole = lax.dynamic_index_in_dim(copies, (rep - p) % 4, 0, keepdims=False)
        cols += [whole[:share], whole[share:]]
    grad_perm = jnp.concatenate([mm(send[h], returned, TN, bf) for h in range(2)], axis=1)
    grad_z = mm(grad_perm, perm, NT, bf)
    return (grad_z[None], jnp.concatenate(cols[:6], axis=1), jnp.concatenate(cols[6:], axis=1))


def solution(mesh):
    rows, reps = mesh.devices.shape
    fine = Mesh(
        mesh.devices.reshape(rows // (Z_HIGH * Z_LOW * CORES), Z_HIGH, Z_LOW, CORES, reps),
        ROWS + ("rep",),
    )
    placed = (
        P("rep", ROWS, None),
        P("rep", ROWS, None),
        P(ROWS, None),
        P(ROWS, None),
        P("rep", ROWS),
        P("rep", ROWS),
    )
    return jax.shard_map(
        per_device,
        mesh=fine,
        in_specs=placed,
        out_specs=(P("rep", ROWS, None), P(ROWS, None), P(ROWS, None)),
        check_vma=False,
    )
```

```python
import jax
import jax.numpy as jnp
from jax import lax
from jax.experimental import pallas as pl
from jax.experimental.pallas import tpu as pltpu
from jax.sharding import Mesh
from jax.sharding import PartitionSpec as P

HEADS = 8
CAP = 2
BLK = 2
Z_HIGH = 4
Z_LOW = 4
CORES = 2
ROWS = ("x", "zh", "zl", "core")
CHIPS = ("x", "zh", "zl")
INTERPRET = False
NN = ((1,), (0,))
NT = ((1,), (1,))
TN = ((0,), (0,))


def mm(left, right, dims, out=jnp.float32):
    res = lax.dot_general(left, right, (dims, ((), ())), preferred_element_type=jnp.float32)
    return res.astype(out)


def rank_within(order_keys, owners):
    same_owner = owners[None, :] == owners[:, None]
    earlier = order_keys[None, :] < order_keys[:, None]
    return jnp.sum(jnp.logical_and(same_owner, earlier).astype(jnp.int32), axis=1)


def slot_table(owners, ranks, count):
    per_chip = CAP * CORES * CORES
    base = (owners * per_chip + ranks) * BLK
    rows = (base[:, None] + jnp.arange(BLK, dtype=jnp.int32)[None, :]).reshape(-1)
    slots = jnp.arange(count * per_chip * BLK, dtype=jnp.int32)
    return (slots[:, None] == rows[None, :]).astype(jnp.bfloat16)


def swap(block, axis):
    return lax.all_to_all(block, axis, split_axis=0, concat_axis=0, tiled=True)


def shift(block, axis, step):
    count = lax.axis_size(axis)
    return lax.ppermute(block, axis, [(here, (here + step) % count) for here in range(count)])


def flip(block, axis, bit):
    count = lax.axis_size(axis)
    return lax.ppermute(block, axis, [(here, here ^ bit) for here in range(count)])


def attend(qkv, grad_attn, own, head_size):
    bf = jnp.bfloat16
    rows = qkv.shape[0]
    scale = head_size ** (-0.5)
    query, key, value = qkv[:, :own], qkv[:, own : 2 * own], qkv[:, 2 * own :]
    key_t, value_t = key.T, value.T
    two = 2 * head_size
    first = lax.broadcasted_iota(jnp.int32, (rows, two), 1) < head_size
    attn_t, dq_t, dk, dv = [], [], [], []
    for pair in range(own // two):
        cols = slice(pair * two, (pair + 1) * two)
        q_pair, k_pair, v_pair, g_pair = query[:, cols], key[:, cols], value[:, cols], grad_attn[:, cols]
        zero = jnp.zeros_like(k_pair)
        dk_pair, dv_pair = [], []
        for member in range(2):
            k_head = jnp.where(first, k_pair, zero) if member == 0 else jnp.where(first, zero, k_pair)
            v_head = jnp.where(first, v_pair, zero) if member == 0 else jnp.where(first, zero, v_pair)
            score = mm(k_head, q_pair, NT)
            raised = jnp.exp((score - jnp.max(score, axis=0, keepdims=True)) * scale)
            probs = raised * (1.0 / jnp.sum(raised, axis=0, keepdims=True))
            probs_b = probs.astype(bf)
            dprob = mm(v_head, g_pair, NT)
            delta = jnp.sum(probs * dprob, axis=0, keepdims=True)
            dscore = (probs * (dprob - delta) * scale).astype(bf)
            lo = pair * two + member * head_size
            attn_t.append(mm(value_t[lo : lo + head_size], probs_b, NN, bf))
            dq_t.append(mm(key_t[lo : lo + head_size], dscore, NN, bf))
            dk_pair.append(mm(dscore, q_pair, NN))
            dv_pair.append(mm(probs_b, g_pair, NN))
        dk.append(jnp.where(first, dk_pair[0], dk_pair[1]).astype(bf))
        dv.append(jnp.where(first, dv_pair[0], dv_pair[1]).astype(bf))
    grad_q = jnp.concatenate(dq_t, axis=0).T
    return jnp.concatenate(attn_t, axis=0), jnp.concatenate([grad_q] + dk + dv, axis=1)


def patch_body(
    place_ref, x_ref, w0_ref, w1_ref, w2_ref, w3_ref, gleft_ref, gright_ref, own_perm_ref,
    pown_ref, poth_ref, keep_ref, send_ref, w_ref, tq_ref, tp_ref,
):
    bf = jnp.bfloat16
    core, rep = place_ref[0], place_ref[1]
    channels = x_ref.shape[1]
    own = channels // CORES
    part = own // CORES
    for k, ref in enumerate((w0_ref, w1_ref, w2_ref, w3_ref)):
        slot = lax.rem(rep + 4 - k, 4)
        w_ref[slot, core] = ref[:own]
        w_ref[slot, 1 - core] = ref[own:]
    w_qkv = jnp.concatenate([w_ref[p].reshape(channels, own) for p in range(3)], axis=1)
    cols = [
        jnp.concatenate([w_ref[3, c, h * part : (h + 1) * part] for c in range(CORES)], axis=0) for h in range(2)
    ]
    own_perm = own_perm_ref[...]
    w_proj = mm(own_perm, jnp.concatenate(cols, axis=1), NN, bf)
    x = x_ref[...]
    grad_pair = jnp.concatenate([gleft_ref[...], gright_ref[...]], axis=1)
    qkv = mm(x, w_qkv, NN, bf)
    grad_attn = mm(grad_pair, w_proj, NT, bf)
    attn_t, grad_qkv = attend(qkv, grad_attn, own, channels // HEADS)
    tq_ref[...] = mm(x, grad_qkv, TN, bf).reshape(CORES, own, 3 * own)
    proj_term = mm(attn_t, grad_pair, NN, bf)
    tp_ref[...] = mm(own_perm, proj_term, TN, bf).reshape(CORES, part, channels)
    for out_ref, side in ((keep_ref, core), (send_ref, 1 - core)):
        out_ref[:, : 3 * own] = tq_ref[side]
        out_ref[:part, 3 * own :] = tp_ref[side, :, :own]
        out_ref[part:, 3 * own :] = tp_ref[side, :, own:]
    partial = mm(grad_qkv, w_qkv, NT)
    left, right = partial[:, :own], partial[:, own:]
    pown_ref[...] = jnp.where(core == 0, left, right)
    poth_ref[...] = jnp.where(core == 0, right, left).astype(bf)


def patch_step(place, x, weights, gleft, gright, own_perm):
    bf = jnp.bfloat16
    rows, own = gleft.shape
    channels = own * CORES
    vmem = pl.BlockSpec(memory_space=pltpu.VMEM)
    return pl.pallas_call(
        patch_body,
        out_shape=[
            jax.ShapeDtypeStruct((rows, own), jnp.float32),
            jax.ShapeDtypeStruct((rows, own), bf),
            jax.ShapeDtypeStruct((own, 4 * own), bf),
            jax.ShapeDtypeStruct((own, 4 * own), bf),
        ],
        in_specs=[pl.BlockSpec(memory_space=pltpu.SMEM)] + [vmem] * 8,
        out_specs=[vmem] * 4,
        scratch_shapes=[
            pltpu.VMEM((4, CORES, own, own), bf),
            pltpu.VMEM((CORES, own, 3 * own), bf),
            pltpu.VMEM((CORES, own // CORES, channels), bf),
        ],
        compiler_params=pltpu.CompilerParams(vmem_limit_bytes=48 << 20),
        interpret=INTERPRET,
    )(place, x, *weights, gleft, gright, own_perm)


def per_device(feats, grad_out, qkv_weight, proj_weight, to_hilbert, to_zorder):
    bf = jnp.bfloat16
    f32 = jnp.float32
    nx, zh, zl, nc, nr = (lax.axis_size(a) for a in ROWS + ("rep",))
    nz = zh * zl
    chips = nx * nz
    x_here, core, rep = (lax.axis_index(a) for a in ("x", "core", "rep"))
    feature = feats[0]
    rows_dev, channels = feature.shape
    own = channels // nc
    part = own // nc
    half = channels // 2
    share = qkv_weight.shape[0]
    blocks_dev = to_hilbert.shape[1]
    chunk = CAP * nc * nc * BLK
    pair = [(0, 1), (1, 0)]
    bits = [1 << b for b in range(nx.bit_length() - 1)]

    mine = lax.dynamic_slice_in_dim(jnp.concatenate([qkv_weight, proj_weight], axis=1), rep * channels, channels, 1)
    mine = jnp.concatenate([mine[:, :own], mine[:, own:]], axis=0)
    plane = swap(jnp.broadcast_to(mine[None], (nz, 2 * share, own)), ("zh", "zl")).reshape(nz * 2 * share, own)

    def both(block):
        theirs = lax.ppermute(block, "core", pair)
        return jnp.where(core == 0, block, theirs), jnp.where(core == 0, theirs, block)

    lists = jnp.stack([to_hilbert[0], to_zorder[0]])
    lists = jnp.concatenate(both(lists), axis=1)
    forward_list, inverse_list = lists[0], lists[1]
    ids = jnp.arange(nc * blocks_dev, dtype=jnp.int32)
    target = forward_list // (nc * blocks_dev)
    send = slot_table(target, rank_within(ids, target), chips)
    source = inverse_list // (nc * blocks_dev)
    recv = slot_table(source, rank_within(inverse_list, source), chips)
    left, right = grad_out[0][:, :half], grad_out[0][:, half:]
    stay = jnp.where(core == 0, left, right)
    come = lax.ppermute(jnp.where(core == 0, right, left), "core", pair)
    grad_z_in = jnp.concatenate([jnp.where(core == 0, stay, come), jnp.where(core == 0, come, stay)], axis=0)
    outgoing = mm(send, grad_z_in, NN, bf)
    outgoing, plane = lax.optimization_barrier((outgoing, plane))
    arrived = swap(outgoing.reshape(chips, chunk, half), CHIPS).reshape(chips * chunk, half)

    gathered = plane
    for bit in bits[::-1]:
        gathered = jnp.concatenate([gathered, flip(gathered, "x", bit)], axis=0)

    def x_index(x):
        apart = x ^ x_here
        index = jnp.zeros_like(apart)
        for bit in bits:
            index = index * 2 + (apart // bit) % 2
        return index

    a = jnp.arange(own, dtype=jnp.int32)
    i_of, z_of, top = a % share, a // share % nz, a // (share * nz)
    slot = jnp.arange(2 * own, dtype=jnp.int32)
    picked = []
    for c in range(nc):
        side = nx // nc
        for_qkv = (x_index(top) * nz + z_of) * 2 + c
        for_proj = (x_index(c * side + top % side) * nz + z_of) * 2 + top // side
        place = jnp.where(rep == 3, for_proj, for_qkv) * share + i_of
        picked.append(mm((place[:, None] == slot[None, :]).astype(bf), gathered, NN, bf))
    kept = jnp.where(core == 0, picked[0], picked[1])
    theirs = lax.ppermute(jnp.where(core == 0, picked[1], picked[0]), "core", pair)
    parts = jnp.concatenate([kept, theirs], axis=0)
    weights = [parts] + [shift(parts, "rep", k) for k in range(1, nr)]
    weights[1], weights[2], weights[3], arrived = lax.optimization_barrier((*weights[1:], arrived))

    def order(count):
        nat = jnp.arange(count, dtype=jnp.int32)
        i, c, z, x = nat % share, nat // share % nc, nat // (share * nc) % nz, nat // (share * nc * nz)
        pos = c * (count // nc) + (x * nz + z) * share + i
        return (pos[:, None] == nat[None, :]).astype(bf)

    perm = order(channels)
    own_perm = order(own)
    x_pair = mm(jnp.concatenate(both(feature), axis=0), perm, NN, bf)
    grad_left, grad_right = both(mm(recv, arrived, TN, bf))
    place = jnp.stack([core, rep])
    p_own, p_other, keep, away = patch_step(place, x_pair, weights, grad_left, grad_right, own_perm)

    from_other = lax.ppermute(p_other, "core", pair)
    grad_hfeat = (p_own + from_other.astype(f32)).astype(bf)
    going = mm(recv, grad_hfeat, NN, bf)
    returned = swap(going.reshape(chips, chunk, half), CHIPS).reshape(chips * chunk, half)

    got = lax.ppermute(away, "core", pair)
    proj = [jnp.concatenate([m[:part, 3 * own :], m[part:, 3 * own :]], axis=1) for m in (keep, got)]
    proj = jnp.concatenate([jnp.where(core == 0, proj[0], proj[1]), jnp.where(core == 0, proj[1], proj[0])], axis=0)
    total = jnp.concatenate([keep[:, : 3 * own], got[:, : 3 * own], proj], axis=1)

    def halve(value, axis, here, bit, first, second):
        mine_set = here // bit % 2 == 1
        stay = jnp.where(mine_set, second, first)
        come = flip(jnp.where(mine_set, first, second), axis, bit)
        return (stay.astype(f32) + come.astype(f32)).astype(bf)

    wide = total.shape[1] // 2
    total = halve(total, "rep", rep, 1, total[:, :wide], total[:, wide:])
    for bit in bits:
        count = nx // bit
        blocks = total.reshape(count // 2, 2, nz * share, total.shape[1])
        flat = (count // 2 * nz * share, total.shape[1])
        total = halve(total, "x", x_here, bit, blocks[:, 0].reshape(flat), blocks[:, 1].reshape(flat))
    total, returned = lax.optimization_barrier((total, returned))
    far = swap(total.reshape(nz, share, wide), ("zh", "zl"))
    summed = jnp.sum(far.astype(f32), axis=0)
    last = swap(jnp.broadcast_to(summed[None], (nr, share, wide)), "rep")
    last = jnp.concatenate([last[0] + last[2], last[1] + last[3]], axis=1)
    grad_half = mm(send, returned, TN, bf)
    stay = jnp.where(core == 0, grad_half[:rows_dev], grad_half[rows_dev:])
    come = lax.ppermute(jnp.where(core == 0, grad_half[rows_dev:], grad_half[:rows_dev]), "core", pair)
    grad_perm = jnp.concatenate([jnp.where(core == 0, stay, come), jnp.where(core == 0, come, stay)], axis=1)
    grad_z = mm(grad_perm, perm, NT, bf)
    lower = jnp.where(core == 0, last[:, : 3 * own], last[:, 3 * own : 6 * own])
    upper = jnp.where(core == 0, last[:, 3 * own : 6 * own], last[:, : 3 * own])
    cols = []
    for p in range(3):
        cols += [lower[:, p * own : (p + 1) * own], upper[:, p * own : (p + 1) * own]]
    return (grad_z[None], jnp.concatenate(cols, axis=1), last[:, 6 * own :])


def solution(mesh):
    rows, reps = mesh.devices.shape
    fine = Mesh(
        mesh.devices.reshape(rows // (Z_HIGH * Z_LOW * CORES), Z_HIGH, Z_LOW, CORES, reps),
        ROWS + ("rep",),
    )
    placed = (
        P("rep", ROWS, None),
        P("rep", ROWS, None),
        P(ROWS, None),
        P(ROWS, None),
        P("rep", ROWS),
        P("rep", ROWS),
    )
    return jax.shard_map(
        per_device,
        mesh=fine,
        in_specs=placed,
        out_specs=(P("rep", ROWS, None), P(ROWS, None), P(ROWS, None)),
        check_vma=False,
    )
```

```python
import jax
import jax.numpy as jnp
from jax import lax
from jax.experimental import pallas as pl
from jax.experimental.pallas import tpu as pltpu
from jax.sharding import Mesh
from jax.sharding import PartitionSpec as P

HEADS = 8
CAP = 2
BLK = 2
Z_HIGH = 4
Z_LOW = 4
CORES = 2
ROWS = ("x", "zh", "zl", "core")
CHIPS = ("x", "zh", "zl")
INTERPRET = False
NN = ((1,), (0,))
NT = ((1,), (1,))
TN = ((0,), (0,))


def mm(left, right, dims, out=jnp.float32):
    res = lax.dot_general(left, right, (dims, ((), ())), preferred_element_type=jnp.float32)
    return res.astype(out)


def rank_within(order_keys, owners):
    same_owner = owners[None, :] == owners[:, None]
    earlier = order_keys[None, :] < order_keys[:, None]
    return jnp.sum(jnp.logical_and(same_owner, earlier).astype(jnp.int32), axis=1)


def slot_tables(owners, ranks, count):
    base = owners * (2 * CAP * BLK) + ranks * BLK
    rows = (base[:, None] + jnp.arange(BLK, dtype=jnp.int32)[None, :]).reshape(-1)
    slots = jnp.arange(count * 2 * CAP * BLK, dtype=jnp.int32)
    return [
        (slots[:, None] == (rows + half * CAP * BLK)[None, :]).astype(jnp.bfloat16)
        for half in range(2)
    ]


def slot_table(owners, ranks, count):
    per_chip = CAP * CORES * CORES
    base = (owners * per_chip + ranks) * BLK
    rows = (base[:, None] + jnp.arange(BLK, dtype=jnp.int32)[None, :]).reshape(-1)
    slots = jnp.arange(count * per_chip * BLK, dtype=jnp.int32)
    return (slots[:, None] == rows[None, :]).astype(jnp.bfloat16)


def swap(block, axis):
    return lax.all_to_all(block, axis, split_axis=0, concat_axis=0, tiled=True)


def shift(block, axis, step):
    count = lax.axis_size(axis)
    return lax.ppermute(block, axis, [(here, (here + step) % count) for here in range(count)])


def flip(block, axis, bit):
    count = lax.axis_size(axis)
    return lax.ppermute(block, axis, [(here, here ^ bit) for here in range(count)])


def attend(qkv, grad_attn, own, head_size):
    bf = jnp.bfloat16
    rows = qkv.shape[0]
    scale = head_size ** (-0.5)
    query, key, value = qkv[:, :own], qkv[:, own : 2 * own], qkv[:, 2 * own :]
    key_t, value_t = key.T, value.T
    two = 2 * head_size
    first = lax.broadcasted_iota(jnp.int32, (rows, two), 1) < head_size
    attn_t, dq_t, dk, dv = [], [], [], []
    for pair in range(own // two):
        cols = slice(pair * two, (pair + 1) * two)
        q_pair, k_pair, v_pair, g_pair = query[:, cols], key[:, cols], value[:, cols], grad_attn[:, cols]
        zero = jnp.zeros_like(k_pair)
        dk_pair, dv_pair = [], []
        for member in range(2):
            k_head = jnp.where(first, k_pair, zero) if member == 0 else jnp.where(first, zero, k_pair)
            v_head = jnp.where(first, v_pair, zero) if member == 0 else jnp.where(first, zero, v_pair)
            score = mm(k_head, q_pair, NT)
            raised = jnp.exp((score - jnp.max(score, axis=0, keepdims=True)) * scale)
            probs = raised * (1.0 / jnp.sum(raised, axis=0, keepdims=True))
            probs_b = probs.astype(bf)
            dprob = mm(v_head, g_pair, NT)
            delta = jnp.sum(probs * dprob, axis=0, keepdims=True)
            dscore = (probs * (dprob - delta) * scale).astype(bf)
            lo = pair * two + member * head_size
            attn_t.append(mm(value_t[lo : lo + head_size], probs_b, NN, bf))
            dq_t.append(mm(key_t[lo : lo + head_size], dscore, NN, bf))
            dk_pair.append(mm(dscore, q_pair, NN))
            dv_pair.append(mm(probs_b, g_pair, NN))
        dk.append(jnp.where(first, dk_pair[0], dk_pair[1]).astype(bf))
        dv.append(jnp.where(first, dv_pair[0], dv_pair[1]).astype(bf))
    grad_q = jnp.concatenate(dq_t, axis=0).T
    return jnp.concatenate(attn_t, axis=0), jnp.concatenate([grad_q] + dk + dv, axis=1)


def patch_body(
    place_ref, x_ref, w0_ref, w1_ref, w2_ref, w3_ref, gown_ref, goth_ref, own_perm_ref,
    pown_ref, poth_ref, keep_ref, send_ref, w_ref, tq_ref, tp_ref,
):
    bf = jnp.bfloat16
    core, rep = place_ref[0], place_ref[1]
    channels = x_ref.shape[1]
    own = channels // CORES
    rows = gown_ref.shape[0]
    part = own // CORES
    for k, ref in enumerate((w0_ref, w1_ref, w2_ref, w3_ref)):
        slot = lax.rem(rep + 4 - k, 4)
        w_ref[slot, core] = ref[:own]
        w_ref[slot, 1 - core] = ref[own:]
    w_qkv = jnp.concatenate([w_ref[p].reshape(channels, own) for p in range(3)], axis=1)
    cols = [
        jnp.concatenate([w_ref[3, c, h * part : (h + 1) * part] for c in range(CORES)], axis=0) for h in range(2)
    ]
    own_perm = own_perm_ref[...]
    w_proj = mm(own_perm, jnp.concatenate(cols, axis=1), NN, bf)
    x = x_ref[...]
    grad_pair = jnp.concatenate([gown_ref[...], goth_ref[...]], axis=0)
    qkv = mm(x, w_qkv, NN, bf)
    grad_attn = mm(grad_pair, w_proj, NT, bf)
    attn_t, grad_qkv = attend(qkv, grad_attn, own, channels // HEADS)
    tq_ref[...] = mm(x, grad_qkv, TN, bf).reshape(CORES, own, 3 * own)
    proj_term = mm(attn_t, grad_pair, NN, bf)
    tp_ref[...] = mm(own_perm, proj_term, TN, bf).reshape(CORES, part, channels)
    for out_ref, side in ((keep_ref, core), (send_ref, 1 - core)):
        out_ref[:, : 3 * own] = tq_ref[side]
        out_ref[:part, 3 * own :] = tp_ref[side, :, :own]
        out_ref[part:, 3 * own :] = tp_ref[side, :, own:]
    partial = mm(grad_qkv, w_qkv, NT)
    left, right = partial[:, :own], partial[:, own:]
    pown_ref[...] = jnp.where(core == 0, left, right)
    theirs = jnp.where(core == 0, right, left).astype(bf)
    poth_ref[:rows] = theirs[rows:]
    poth_ref[rows:] = theirs[:rows]


def patch_step(place, x, weights, gown, goth, own_perm):
    bf = jnp.bfloat16
    rows, channels = gown.shape
    own = channels // CORES
    vmem = pl.BlockSpec(memory_space=pltpu.VMEM)
    return pl.pallas_call(
        patch_body,
        out_shape=[
            jax.ShapeDtypeStruct((CORES * rows, own), jnp.float32),
            jax.ShapeDtypeStruct((CORES * rows, own), bf),
            jax.ShapeDtypeStruct((own, 4 * own), bf),
            jax.ShapeDtypeStruct((own, 4 * own), bf),
        ],
        in_specs=[pl.BlockSpec(memory_space=pltpu.SMEM)] + [vmem] * 8,
        out_specs=[vmem] * 4,
        scratch_shapes=[
            pltpu.VMEM((4, CORES, own, own), bf),
            pltpu.VMEM((CORES, own, 3 * own), bf),
            pltpu.VMEM((CORES, own // CORES, channels), bf),
        ],
        compiler_params=pltpu.CompilerParams(vmem_limit_bytes=48 << 20),
        interpret=INTERPRET,
    )(place, x, *weights, gown, goth, own_perm)


def per_device(feats, grad_out, qkv_weight, proj_weight, to_hilbert, to_zorder):
    bf = jnp.bfloat16
    f32 = jnp.float32
    nx, zh, zl, nc, nr = (lax.axis_size(a) for a in ROWS + ("rep",))
    nz = zh * zl
    peers = nx * nz * nc
    x_here, core, rep = (lax.axis_index(a) for a in ("x", "core", "rep"))
    feature = feats[0]
    rows_dev, channels = feature.shape
    own = channels // nc
    part = own // nc
    half = channels // 2
    share = qkv_weight.shape[0]
    blocks_dev = to_hilbert.shape[1]
    chunk = 2 * CAP * BLK
    pair = [(0, 1), (1, 0)]
    bits = [1 << b for b in range(nx.bit_length() - 1)]

    mine = lax.dynamic_slice_in_dim(jnp.concatenate([qkv_weight, proj_weight], axis=1), rep * channels, channels, 1)
    mine = jnp.concatenate([mine[:, :own], mine[:, own:]], axis=0)
    plane = swap(jnp.broadcast_to(mine[None], (nz, 2 * share, own)), ("zh", "zl")).reshape(nz * 2 * share, own)

    ids = jnp.arange(blocks_dev, dtype=jnp.int32)
    target = to_hilbert[0] // blocks_dev
    send = slot_tables(target, rank_within(ids, target), peers)
    source = to_zorder[0] // blocks_dev
    recv = slot_tables(source, rank_within(to_zorder[0], source), peers)
    grad_z_in = grad_out[0]
    outgoing = (mm(send[0], grad_z_in[:, :half], NN) + mm(send[1], grad_z_in[:, half:], NN)).astype(bf)
    outgoing, plane = lax.optimization_barrier((outgoing, plane))
    arrived = swap(outgoing.reshape(peers, chunk, half), ROWS).reshape(peers * chunk, half)

    gathered = plane
    for bit in bits[::-1]:
        gathered = jnp.concatenate([gathered, flip(gathered, "x", bit)], axis=0)

    def x_index(x):
        apart = x ^ x_here
        index = jnp.zeros_like(apart)
        for bit in bits:
            index = index * 2 + (apart // bit) % 2
        return index

    a = jnp.arange(own, dtype=jnp.int32)
    i_of, z_of, top = a % share, a // share % nz, a // (share * nz)
    slot = jnp.arange(2 * own, dtype=jnp.int32)
    picked = []
    for c in range(nc):
        side = nx // nc
        for_qkv = (x_index(top) * nz + z_of) * 2 + c
        for_proj = (x_index(c * side + top % side) * nz + z_of) * 2 + top // side
        place = jnp.where(rep == 3, for_proj, for_qkv) * share + i_of
        picked.append(mm((place[:, None] == slot[None, :]).astype(bf), gathered, NN, bf))
    kept = jnp.where(core == 0, picked[0], picked[1])
    theirs = lax.ppermute(jnp.where(core == 0, picked[1], picked[0]), "core", pair)
    parts = jnp.concatenate([kept, theirs], axis=0)
    weights = [parts] + [shift(parts, "rep", k) for k in range(1, nr)]

    def order(count):
        nat = jnp.arange(count, dtype=jnp.int32)
        i, c, z, x = nat % share, nat // share % nc, nat // (share * nc) % nz, nat // (share * nc * nz)
        pos = c * (count // nc) + (x * nz + z) * share + i
        return (pos[:, None] == nat[None, :]).astype(bf)

    perm = order(channels)
    own_perm = order(own)
    other_feat = lax.ppermute(feature, "core", pair)
    x_pair = mm(jnp.concatenate([feature, other_feat], axis=0), perm, NN, bf)
    grad_hil = jnp.concatenate([mm(recv[h], arrived, TN, bf) for h in range(2)], axis=1)
    other_grad = lax.ppermute(grad_hil, "core", pair)
    place = jnp.stack([core, rep])
    p_own, p_other, keep, away = patch_step(place, x_pair, weights, grad_hil, other_grad, own_perm)

    lists = jnp.stack([to_hilbert[0], to_zorder[0]])
    lists = jnp.concatenate([lists, lax.ppermute(lists, "core", pair)], axis=1)
    keys = jnp.concatenate([ids + core * blocks_dev, ids + (1 - core) * blocks_dev])
    target = lists[0] // (nc * blocks_dev)
    send_chip = slot_table(target, rank_within(keys, target), nx * nz)
    source = lists[1] // (nc * blocks_dev)
    recv_chip = slot_table(source, rank_within(lists[1], source), nx * nz)
    from_other = lax.ppermute(p_other, "core", pair)
    grad_hfeat = (p_own + from_other.astype(f32)).astype(bf)
    going = mm(recv_chip, grad_hfeat, NN, bf)
    returned = swap(going.reshape(nx * nz, -1, half), CHIPS).reshape(-1, half)

    got = lax.ppermute(away, "core", pair)
    proj = [jnp.concatenate([m[:part, 3 * own :], m[part:, 3 * own :]], axis=1) for m in (keep, got)]
    proj = jnp.concatenate([jnp.where(core == 0, proj[0], proj[1]), jnp.where(core == 0, proj[1], proj[0])], axis=0)
    total = jnp.concatenate([keep[:, : 3 * own], got[:, : 3 * own], proj], axis=1)

    def halve(value, axis, here, bit, first, second):
        mine_set = here // bit % 2 == 1
        stay = jnp.where(mine_set, second, first)
        come = flip(jnp.where(mine_set, first, second), axis, bit)
        return (stay.astype(f32) + come.astype(f32)).astype(bf)

    wide = total.shape[1] // 2
    total = halve(total, "rep", rep, 1, total[:, :wide], total[:, wide:])
    for bit in bits:
        count = nx // bit
        blocks = total.reshape(count // 2, 2, nz * share, total.shape[1])
        flat = (count // 2 * nz * share, total.shape[1])
        total = halve(total, "x", x_here, bit, blocks[:, 0].reshape(flat), blocks[:, 1].reshape(flat))
    total, returned = lax.optimization_barrier((total, returned))
    far = swap(total.reshape(nz, share, wide), ("zh", "zl"))
    summed = jnp.sum(far.astype(f32), axis=0)
    last = swap(jnp.broadcast_to(summed[None], (nr, share, wide)), "rep")
    last = jnp.concatenate([last[0] + last[2], last[1] + last[3]], axis=1)
    grad_half = mm(send_chip, returned, TN, bf)
    stay = grad_half[:rows_dev]
    come = lax.ppermute(grad_half[rows_dev:], "core", pair)
    grad_perm = jnp.concatenate([jnp.where(core == 0, stay, come), jnp.where(core == 0, come, stay)], axis=1)
    grad_z = mm(grad_perm, perm, NT, bf)
    lower = jnp.where(core == 0, last[:, : 3 * own], last[:, 3 * own : 6 * own])
    upper = jnp.where(core == 0, last[:, 3 * own : 6 * own], last[:, : 3 * own])
    cols = []
    for p in range(3):
        cols += [lower[:, p * own : (p + 1) * own], upper[:, p * own : (p + 1) * own]]
    return (grad_z[None], jnp.concatenate(cols, axis=1), last[:, 6 * own :])


def solution(mesh):
    rows, reps = mesh.devices.shape
    fine = Mesh(
        mesh.devices.reshape(rows // (Z_HIGH * Z_LOW * CORES), Z_HIGH, Z_LOW, CORES, reps),
        ROWS + ("rep",),
    )
    placed = (
        P("rep", ROWS, None),
        P("rep", ROWS, None),
        P(ROWS, None),
        P(ROWS, None),
        P("rep", ROWS),
        P("rep", ROWS),
    )
    return jax.shard_map(
        per_device,
        mesh=fine,
        in_specs=placed,
        out_specs=(P("rep", ROWS, None), P(ROWS, None), P(ROWS, None)),
        check_vma=False,
    )
```

```python
import jax
import jax.numpy as jnp
from jax import lax
from jax.experimental import pallas as pl
from jax.experimental.pallas import tpu as pltpu
from jax.sharding import Mesh
from jax.sharding import PartitionSpec as P

HEADS = 8
CAP = 2
BLK = 2
Z_HIGH = 4
Z_LOW = 4
CORES = 2
ROWS = ("x", "zh", "zl", "core")
CHIPS = ("x", "zh", "zl")
INTERPRET = False
NN = ((1,), (0,))
NT = ((1,), (1,))
TN = ((0,), (0,))


def mm(left, right, dims, out=jnp.float32):
    res = lax.dot_general(left, right, (dims, ((), ())), preferred_element_type=jnp.float32)
    return res.astype(out)


def rank_within(order_keys, owners):
    same_owner = owners[None, :] == owners[:, None]
    earlier = order_keys[None, :] < order_keys[:, None]
    return jnp.sum(jnp.logical_and(same_owner, earlier).astype(jnp.int32), axis=1)


def slot_tables(owners, ranks, count):
    base = owners * (2 * CAP * BLK) + ranks * BLK
    rows = (base[:, None] + jnp.arange(BLK, dtype=jnp.int32)[None, :]).reshape(-1)
    slots = jnp.arange(count * 2 * CAP * BLK, dtype=jnp.int32)
    return [
        (slots[:, None] == (rows + half * CAP * BLK)[None, :]).astype(jnp.bfloat16)
        for half in range(2)
    ]


def slot_table(owners, ranks, count):
    per_chip = CAP * CORES * CORES
    base = (owners * per_chip + ranks) * BLK
    rows = (base[:, None] + jnp.arange(BLK, dtype=jnp.int32)[None, :]).reshape(-1)
    slots = jnp.arange(count * per_chip * BLK, dtype=jnp.int32)
    return (slots[:, None] == rows[None, :]).astype(jnp.bfloat16)


def swap(block, axis):
    return lax.all_to_all(block, axis, split_axis=0, concat_axis=0, tiled=True)


def shift(block, axis, step):
    count = lax.axis_size(axis)
    return lax.ppermute(block, axis, [(here, (here + step) % count) for here in range(count)])


def flip(block, axis, bit):
    count = lax.axis_size(axis)
    return lax.ppermute(block, axis, [(here, here ^ bit) for here in range(count)])


def attend(qkv, grad_attn, own, head_size):
    bf = jnp.bfloat16
    rows = qkv.shape[0]
    scale = head_size ** (-0.5)
    query, key, value = qkv[:, :own], qkv[:, own : 2 * own], qkv[:, 2 * own :]
    key_t, value_t = key.T, value.T
    two = 2 * head_size
    first = lax.broadcasted_iota(jnp.int32, (rows, two), 1) < head_size
    attn_t, dq_t, dk, dv = [], [], [], []
    for pair in range(own // two):
        cols = slice(pair * two, (pair + 1) * two)
        q_pair, k_pair, v_pair, g_pair = query[:, cols], key[:, cols], value[:, cols], grad_attn[:, cols]
        zero = jnp.zeros_like(k_pair)
        dk_pair, dv_pair = [], []
        for member in range(2):
            k_head = jnp.where(first, k_pair, zero) if member == 0 else jnp.where(first, zero, k_pair)
            v_head = jnp.where(first, v_pair, zero) if member == 0 else jnp.where(first, zero, v_pair)
            score = mm(k_head, q_pair, NT)
            raised = jnp.exp((score - jnp.max(score, axis=0, keepdims=True)) * scale)
            probs = raised * (1.0 / jnp.sum(raised, axis=0, keepdims=True))
            probs_b = probs.astype(bf)
            dprob = mm(v_head, g_pair, NT)
            delta = jnp.sum(probs * dprob, axis=0, keepdims=True)
            dscore = (probs * (dprob - delta) * scale).astype(bf)
            lo = pair * two + member * head_size
            attn_t.append(mm(value_t[lo : lo + head_size], probs_b, NN, bf))
            dq_t.append(mm(key_t[lo : lo + head_size], dscore, NN, bf))
            dk_pair.append(mm(dscore, q_pair, NN))
            dv_pair.append(mm(probs_b, g_pair, NN))
        dk.append(jnp.where(first, dk_pair[0], dk_pair[1]).astype(bf))
        dv.append(jnp.where(first, dv_pair[0], dv_pair[1]).astype(bf))
    grad_q = jnp.concatenate(dq_t, axis=0).T
    return jnp.concatenate(attn_t, axis=0), jnp.concatenate([grad_q] + dk + dv, axis=1)


def patch_body(
    place_ref, x_ref, w0_ref, w1_ref, w2_ref, w3_ref, gown_ref, goth_ref, own_perm_ref,
    pown_ref, poth_ref, keep_ref, send_ref, w_ref, tq_ref, tp_ref,
):
    bf = jnp.bfloat16
    core, rep = place_ref[0], place_ref[1]
    channels = x_ref.shape[1]
    own = channels // CORES
    rows = gown_ref.shape[0]
    part = own // CORES
    for k, ref in enumerate((w0_ref, w1_ref, w2_ref, w3_ref)):
        slot = lax.rem(rep + 4 - k, 4)
        w_ref[slot, core] = ref[:own]
        w_ref[slot, 1 - core] = ref[own:]
    w_qkv = jnp.concatenate([w_ref[p].reshape(channels, own) for p in range(3)], axis=1)
    cols = [
        jnp.concatenate([w_ref[3, c, h * part : (h + 1) * part] for c in range(CORES)], axis=0) for h in range(2)
    ]
    own_perm = own_perm_ref[...]
    w_proj = mm(own_perm, jnp.concatenate(cols, axis=1), NN, bf)
    x = x_ref[...]
    grad_pair = jnp.concatenate([gown_ref[...], goth_ref[...]], axis=0)
    qkv = mm(x, w_qkv, NN, bf)
    grad_attn = mm(grad_pair, w_proj, NT, bf)
    attn_t, grad_qkv = attend(qkv, grad_attn, own, channels // HEADS)
    tq_ref[...] = mm(x, grad_qkv, TN, bf).reshape(CORES, own, 3 * own)
    proj_term = mm(attn_t, grad_pair, NN, bf)
    tp_ref[...] = mm(own_perm, proj_term, TN, bf).reshape(CORES, part, channels)
    for out_ref, side in ((keep_ref, core), (send_ref, 1 - core)):
        out_ref[:, : 3 * own] = tq_ref[side]
        out_ref[:part, 3 * own :] = tp_ref[side, :, :own]
        out_ref[part:, 3 * own :] = tp_ref[side, :, own:]
    partial = mm(grad_qkv, w_qkv, NT)
    left, right = partial[:, :own], partial[:, own:]
    pown_ref[...] = jnp.where(core == 0, left, right)
    theirs = jnp.where(core == 0, right, left).astype(bf)
    poth_ref[:rows] = theirs[rows:]
    poth_ref[rows:] = theirs[:rows]


def patch_step(place, x, weights, gown, goth, own_perm):
    bf = jnp.bfloat16
    rows, channels = gown.shape
    own = channels // CORES
    vmem = pl.BlockSpec(memory_space=pltpu.VMEM)
    return pl.pallas_call(
        patch_body,
        out_shape=[
            jax.ShapeDtypeStruct((CORES * rows, own), jnp.float32),
            jax.ShapeDtypeStruct((CORES * rows, own), bf),
            jax.ShapeDtypeStruct((own, 4 * own), bf),
            jax.ShapeDtypeStruct((own, 4 * own), bf),
        ],
        in_specs=[pl.BlockSpec(memory_space=pltpu.SMEM)] + [vmem] * 8,
        out_specs=[vmem] * 4,
        scratch_shapes=[
            pltpu.VMEM((4, CORES, own, own), bf),
            pltpu.VMEM((CORES, own, 3 * own), bf),
            pltpu.VMEM((CORES, own // CORES, channels), bf),
        ],
        compiler_params=pltpu.CompilerParams(vmem_limit_bytes=48 << 20),
        interpret=INTERPRET,
    )(place, x, *weights, gown, goth, own_perm)


def per_device(feats, grad_out, qkv_weight, proj_weight, to_hilbert, to_zorder):
    bf = jnp.bfloat16
    f32 = jnp.float32
    nx, zh, zl, nc, nr = (lax.axis_size(a) for a in ROWS + ("rep",))
    nz = zh * zl
    peers = nx * nz * nc
    x_here, core, rep = (lax.axis_index(a) for a in ("x", "core", "rep"))
    feature = feats[0]
    rows_dev, channels = feature.shape
    own = channels // nc
    part = own // nc
    half = channels // 2
    share = qkv_weight.shape[0]
    blocks_dev = to_hilbert.shape[1]
    chunk = 2 * CAP * BLK
    pair = [(0, 1), (1, 0)]
    bits = [1 << b for b in range(nx.bit_length() - 1)]

    mine = lax.dynamic_slice_in_dim(jnp.concatenate([qkv_weight, proj_weight], axis=1), rep * channels, channels, 1)
    mine = jnp.concatenate([mine[:, :own], mine[:, own:]], axis=0)
    plane = swap(jnp.broadcast_to(mine[None], (nz, 2 * share, own)), ("zh", "zl")).reshape(nz * 2 * share, own)

    ids = jnp.arange(blocks_dev, dtype=jnp.int32)
    target = to_hilbert[0] // blocks_dev
    send = slot_tables(target, rank_within(ids, target), peers)
    source = to_zorder[0] // blocks_dev
    recv = slot_tables(source, rank_within(to_zorder[0], source), peers)
    grad_z_in = grad_out[0]
    outgoing = (mm(send[0], grad_z_in[:, :half], NN) + mm(send[1], grad_z_in[:, half:], NN)).astype(bf)
    outgoing, plane = lax.optimization_barrier((outgoing, plane))
    arrived = swap(outgoing.reshape(peers, chunk, half), ROWS).reshape(peers * chunk, half)

    gathered = plane
    for bit in bits[::-1]:
        gathered = jnp.concatenate([gathered, flip(gathered, "x", bit)], axis=0)

    def x_index(x):
        apart = x ^ x_here
        index = jnp.zeros_like(apart)
        for bit in bits:
            index = index * 2 + (apart // bit) % 2
        return index

    a = jnp.arange(own, dtype=jnp.int32)
    i_of, z_of, top = a % share, a // share % nz, a // (share * nz)
    slot = jnp.arange(2 * own, dtype=jnp.int32)
    picked = []
    for c in range(nc):
        side = nx // nc
        for_qkv = (x_index(top) * nz + z_of) * 2 + c
        for_proj = (x_index(c * side + top % side) * nz + z_of) * 2 + top // side
        place = jnp.where(rep == 3, for_proj, for_qkv) * share + i_of
        picked.append(mm((place[:, None] == slot[None, :]).astype(bf), gathered, NN, bf))
    kept = jnp.where(core == 0, picked[0], picked[1])
    theirs = lax.ppermute(jnp.where(core == 0, picked[1], picked[0]), "core", pair)
    parts = jnp.concatenate([kept, theirs], axis=0)
    sent = {k: shift(parts, "rep", k) for k in (2, 1, 3)}
    weights = [parts] + [sent[k] for k in range(1, nr)]

    def order(count):
        nat = jnp.arange(count, dtype=jnp.int32)
        i, c, z, x = nat % share, nat // share % nc, nat // (share * nc) % nz, nat // (share * nc * nz)
        pos = c * (count // nc) + (x * nz + z) * share + i
        return (pos[:, None] == nat[None, :]).astype(bf)

    perm = order(channels)
    own_perm = order(own)
    other_feat = lax.ppermute(feature, "core", pair)
    x_pair = mm(jnp.concatenate([feature, other_feat], axis=0), perm, NN, bf)
    grad_hil = jnp.concatenate([mm(recv[h], arrived, TN, bf) for h in range(2)], axis=1)
    other_grad = lax.ppermute(grad_hil, "core", pair)
    place = jnp.stack([core, rep])
    p_own, p_other, keep, away = patch_step(place, x_pair, weights, grad_hil, other_grad, own_perm)

    lists = jnp.stack([to_hilbert[0], to_zorder[0]])
    lists = jnp.concatenate([lists, lax.ppermute(lists, "core", pair)], axis=1)
    keys = jnp.concatenate([ids + core * blocks_dev, ids + (1 - core) * blocks_dev])
    target = lists[0] // (nc * blocks_dev)
    send_chip = slot_table(target, rank_within(keys, target), nx * nz)
    source = lists[1] // (nc * blocks_dev)
    recv_chip = slot_table(source, rank_within(lists[1], source), nx * nz)
    from_other = lax.ppermute(p_other, "core", pair)
    grad_hfeat = (p_own + from_other.astype(f32)).astype(bf)
    going = mm(recv_chip, grad_hfeat, NN, bf)
    returned = swap(going.reshape(nx * nz, -1, half), CHIPS).reshape(-1, half)

    got = lax.ppermute(away, "core", pair)
    proj = [jnp.concatenate([m[:part, 3 * own :], m[part:, 3 * own :]], axis=1) for m in (keep, got)]
    proj = jnp.concatenate([jnp.where(core == 0, proj[0], proj[1]), jnp.where(core == 0, proj[1], proj[0])], axis=0)
    total = jnp.concatenate([keep[:, : 3 * own], got[:, : 3 * own], proj], axis=1)

    def halve(value, axis, here, bit, first, second):
        mine_set = here // bit % 2 == 1
        stay = jnp.where(mine_set, second, first)
        come = flip(jnp.where(mine_set, first, second), axis, bit)
        return (stay.astype(f32) + come.astype(f32)).astype(bf)

    wide = total.shape[1] // 2
    total = halve(total, "rep", rep, 1, total[:, :wide], total[:, wide:])
    for bit in bits:
        count = nx // bit
        blocks = total.reshape(count // 2, 2, nz * share, total.shape[1])
        flat = (count // 2 * nz * share, total.shape[1])
        total = halve(total, "x", x_here, bit, blocks[:, 0].reshape(flat), blocks[:, 1].reshape(flat))
    total, returned = lax.optimization_barrier((total, returned))
    far = swap(total.reshape(nz, share, wide), ("zh", "zl"))
    summed = jnp.sum(far.astype(f32), axis=0)
    last = swap(jnp.broadcast_to(summed[None], (nr, share, wide)), "rep")
    last = jnp.concatenate([last[0] + last[2], last[1] + last[3]], axis=1)
    grad_half = mm(send_chip, returned, TN, bf)
    stay = grad_half[:rows_dev]
    come = lax.ppermute(grad_half[rows_dev:], "core", pair)
    grad_perm = jnp.concatenate([jnp.where(core == 0, stay, come), jnp.where(core == 0, come, stay)], axis=1)
    grad_z = mm(grad_perm, perm, NT, bf)
    lower = jnp.where(core == 0, last[:, : 3 * own], last[:, 3 * own : 6 * own])
    upper = jnp.where(core == 0, last[:, 3 * own : 6 * own], last[:, : 3 * own])
    cols = []
    for p in range(3):
        cols += [lower[:, p * own : (p + 1) * own], upper[:, p * own : (p + 1) * own]]
    return (grad_z[None], jnp.concatenate(cols, axis=1), last[:, 6 * own :])


def solution(mesh):
    rows, reps = mesh.devices.shape
    fine = Mesh(
        mesh.devices.reshape(rows // (Z_HIGH * Z_LOW * CORES), Z_HIGH, Z_LOW, CORES, reps),
        ROWS + ("rep",),
    )
    placed = (
        P("rep", ROWS, None),
        P("rep", ROWS, None),
        P(ROWS, None),
        P(ROWS, None),
        P("rep", ROWS),
        P("rep", ROWS),
    )
    return jax.shard_map(
        per_device,
        mesh=fine,
        in_specs=placed,
        out_specs=(P("rep", ROWS, None), P(ROWS, None), P(ROWS, None)),
        check_vma=False,
    )
```
